256 devices in a mesh: row: 8 (over y, core), col: 32 (over x, z).
Axes of the slice: x: 4, y: 4, z: 8, core: 2. Of those that a mesh axis runs over, the one named last changes fastest.
Arguments:
- object_field: float32 [2, 2048, 8192], P(None, 'row', 'col'), may hold values from -6 to 6
- probe_field: float32 [2, 2, 128, 128], replicated, may hold values from -6 to 6
- amplitudes: float32 [8, 32, 24, 128, 128], P('row', 'col'), may hold values from 0.3 to 6
- offsets: int32 [8, 32, 24, 2], P('row', 'col'), may hold values from -64 to 191
- counts: int32 [8, 32], P('row', 'col'), may hold values from 1 to 24, as said below
Outputs:
- object_next: float32 [2, 2048, 8192], P(None, 'row', 'col')
- probe_next: float32 [2, 2, 128, 128], replicated
The draws below stay inside these ranges and needn't reach their ends.
Inputs may be any that keep to these rules, and one draw needn't show every extreme that they name: `counts`: slots at and above a tile's count are unused; some tile has all 24 slots live.
All inputs are finite; a program needn't handle non-finite values.
Results may differ from the reference program's by a relative error of at most 0.0001.
Values sent between devices are 32-bit elements; how exact they have to be, the bound alone decides.
A program may use at most 64 MiB of HBM per device.

```python
import math
import jax
import jax.numpy as jnp
from jax import lax

PSIZE = 128
MODES = 2
PASSES = 2
TILE = 256
CAP = 24
HALF = 64
NR = 2048
NC = 8192
SLOTS = 6144
N_ROW = 8
N_COL = 32


def draw_counts(key, part):
    col_index = jnp.arange(N_COL, dtype=jnp.int32)
    ceiling = (CAP + 2 * CAP * col_index // max(N_COL - 1, 1)) // 3
    ceiling = jnp.maximum(ceiling, 1)
    first_key = jax.random.fold_in(key, 11)
    second_key = jax.random.fold_in(key, 23)
    drawn = jax.random.randint(first_key, (N_ROW, N_COL), 0, 1 << 20)
    result = 1 + drawn % ceiling[None, :]
    chosen = jax.random.randint(second_key, (), 0, N_ROW)
    return result.at[chosen, N_COL - 1].set(CAP).astype(jnp.int32)


def with_ends(values, key, smallest, top_value):
    spot = [jax.random.randint(jax.random.fold_in(key, axis), (), 0, length) for axis, length in enumerate(values.shape)]
    longest = values.shape.index(max(values.shape))
    next_to = spot[:longest] + [(spot[longest] + 1) % values.shape[longest]] + spot[longest + 1:]
    return values.at[tuple(spot)].set(smallest).at[tuple(next_to)].set(top_value)


def steps_of(key, extent, pieces, low, largest):
    level, own = 1.0, jax.random.fold_in(key, 6)
    for dim, shards_of in pieces:
        draws = jnp.exp(jax.random.uniform(jax.random.fold_in(own, dim), (shards_of,), jnp.float32, low / len(pieces), largest / len(pieces)))
        level = level * jnp.repeat(draws, extent[dim] // shards_of).reshape([-1 if axis == dim else 1 for axis in range(len(extent))])
    return level


def centred(rng, dims, width, reach, cuts=(), kind=jnp.bfloat16):
    loudness = steps_of(rng, dims, cuts, -0.22, 0.18) if cuts else 1.0
    values = jax.random.normal(rng, dims, jnp.float32) * width * loudness
    return jnp.minimum(jnp.maximum(values, -reach), reach).astype(kind)


def setup_inputs(seed: int = 0) -> dict:
    key_list = jax.random.split(jax.random.key(seed), 6)
    object_field = centred(key_list[0], (2, NR, NC), 1.0, 6.0, ((1, 8), (2, 32)), jnp.float32)
    probe_field = centred(key_list[1], (2, MODES, PSIZE, PSIZE), 1.0, 6.0, (), jnp.float32)
    amplitudes = jnp.clip(jnp.exp(math.log(6.0) - 2.9957322 * jax.random.uniform(key_list[2], (N_ROW, N_COL, CAP, PSIZE, PSIZE), jnp.float32) ** steps_of(key_list[2], (N_ROW, N_COL, CAP, PSIZE, PSIZE), ((0, 8), (1, 32)), -0.2, 0.2)), 0.3, 6.0)
    offsets = with_ends(jax.random.randint(key_list[3], (N_ROW, N_COL, CAP, 2), 0 - HALF, TILE - HALF), jax.random.fold_in(key_list[3], 1), 0 - HALF, (TILE - HALF) - 1).astype(jnp.int32)
    counts = draw_counts(jax.random.fold_in(key_list[5], 71), 0)
    return dict(object_field=object_field, probe_field=probe_field, amplitudes=amplitudes, offsets=offsets, counts=counts)


EPSILON = 1e-06

def exit_change(window, probe, amplitude):
    psi = probe * window[None]
    spectrum = jnp.fft.fft2(psi, norm='ortho')
    total = lax.optimization_barrier(jnp.sum(jnp.real(spectrum) ** 2 + jnp.imag(spectrum) ** 2, axis=0))
    factor = amplitude / jnp.maximum(jnp.sqrt(total), 1.0)
    revised = jnp.fft.ifft2(spectrum * factor[None], norm='ortho')
    return revised - psi

def reference(object_field, probe_field, amplitudes, offsets, counts):
    probe = lax.complex(probe_field[0], probe_field[1])
    power = lax.optimization_barrier(jnp.sum(probe_field[0] ** 2 + probe_field[1] ** 2, axis=0))
    regular = 0.1 * jnp.max(power) + EPSILON
    slot_index = jnp.arange(CAP, dtype=jnp.int32)
    live = (slot_index[None, None, :] < counts[:, :, None]).astype(power.dtype)
    tile_rows = (jnp.arange(N_ROW, dtype=jnp.int32) * TILE)[:, None, None]
    tile_cols = (jnp.arange(N_COL, dtype=jnp.int32) * TILE)[None, :, None]
    start_rows = (offsets[..., 0] + tile_rows + HALF).reshape(-1).astype(jnp.int32)
    start_cols = (offsets[..., 1] + tile_cols + HALF).reshape(-1).astype(jnp.int32)
    flat_amps = amplitudes.reshape(-1, PSIZE, PSIZE)
    flat_live = live.reshape(-1)
    current = object_field
    gradient = jnp.zeros_like(probe)
    for pass_index in range(PASSES):
        padded = jnp.pad(current, ((0, 0), (HALF, HALF), (HALF, HALF)))
        numer_init = jnp.zeros((3,) + padded.shape[1:], power.dtype)

        def visit(carry, item):
            numer, grad = carry
            row_start, col_start, amplitude, alive = item
            zero = jnp.zeros((), jnp.int32)
            block = lax.dynamic_slice(padded, (zero, row_start, col_start), (2, PSIZE, PSIZE))
            window = lax.complex(block[0], block[1])
            change = exit_change(window, probe, amplitude) * alive
            object_term = lax.optimization_barrier(jnp.sum(jnp.conj(probe) * change, axis=0))
            patch = jnp.stack([jnp.real(object_term), jnp.imag(object_term), power * alive])
            before = lax.dynamic_slice(numer, (zero, row_start, col_start), (3, PSIZE, PSIZE))
            numer = lax.dynamic_update_slice(numer, before + patch, (zero, row_start, col_start))
            mean_power = jnp.mean(block[0] ** 2 + block[1] ** 2) + EPSILON
            grad = grad + jnp.conj(window)[None] * change / mean_power
            return ((numer, grad), None)
        (numer, gradient), _ = lax.scan(visit, (numer_init, gradient), (start_rows, start_cols, flat_amps, flat_live))
        inner = numer[:, HALF:HALF + NR, HALF:HALF + NC]
        current = current + inner[:2] / (inner[2:3] + regular)
    probe_new = probe + gradient / SLOTS
    return (current, jnp.stack([jnp.real(probe_new), jnp.imag(probe_new)]))
```

```python
import functools

import jax
import jax.numpy as jnp
import ml_dtypes
import numpy as np
from jax import lax
from jax.experimental import pallas as pl
from jax.experimental.pallas import tpu as pltpu
from jax.sharding import PartitionSpec as P

F32 = jnp.float32
BF16 = jnp.bfloat16
EPSILON = 1e-06
MESH = pl.DeviceIdType.MESH
VMEM = pl.BlockSpec(memory_space=pltpu.VMEM)
SMEM = pl.BlockSpec(memory_space=pltpu.SMEM)

SIZE = 128
TILE = 256
HALF = 64
EXT = TILE + 2 * HALF
ROWS, COLS = 8, 32
XS, YS, ZS = 4, 4, 8
UNROLL = 4

DIRS = [(-1, 0), (1, 0), (0, -1), (0, 1), (-1, -1), (-1, 1), (1, -1), (1, 1)]


def dft_tables():
    k = np.arange(SIZE)
    angles = 2 * np.pi / SIZE * ((k[:, None] * k[None, :]) % SIZE)
    c, s = np.cos(angles) / np.sqrt(SIZE), np.sin(angles) / np.sqrt(SIZE)
    terms = []
    for table in (np.block([[c, -s], [s, c]]), np.block([[c, s], [-s, c]])):
        high = table.astype(ml_dtypes.bfloat16)
        low = (table - high.astype(np.float64)).astype(ml_dtypes.bfloat16)
        terms += [high, low]
    return np.stack(terms)


def half_turn(x):
    return pltpu.roll(x, HALF, 1)


def lanes(rows):
    return lax.broadcasted_iota(jnp.int32, (rows, SIZE), 1)


def neighbour(direction):
    row = lax.axis_index("row") + direction[0]
    col = lax.axis_index("col") + direction[1]
    valid = (row >= 0) & (row < ROWS) & (col >= 0) & (col < COLS)
    return (row, col), valid


def signal_neighbours(barrier):
    count = jnp.int32(0)
    for direction in DIRS:
        where, valid = neighbour(direction)

        @pl.when(valid)
        def _():
            pl.semaphore_signal(barrier, 1, device_id=where, device_id_type=MESH)

        count = count + valid.astype(jnp.int32)
    return count


class Exchange:
    def __init__(self, dsts, send, recv):
        self.dsts, self.send, self.recv = dsts, send, recv

    def copy(self, k, src, where):
        return pltpu.make_async_remote_copy(
            src, self.dsts[k], self.send.at[k], self.recv.at[k], device_id=where, device_id_type=MESH
        )

    def start(self, k, src):
        where, valid = neighbour(DIRS[k])

        @pl.when(valid)
        def _():
            self.copy(k, src, where).start()

    def clear_missing(self):
        for k, (dr, dc) in enumerate(DIRS):
            _, valid = neighbour((-dr, -dc))

            @pl.when(jnp.logical_not(valid))
            def _():
                self.dsts[k][...] = jnp.zeros_like(self.dsts[k])

    def wait_recv(self, k):
        where, valid = neighbour((-DIRS[k][0], -DIRS[k][1]))

        @pl.when(valid)
        def _():
            self.copy(k, self.dsts[k], where).wait_recv()

    def wait_send(self, k, src):
        where, valid = neighbour(DIRS[k])

        @pl.when(valid)
        def _():
            self.copy(k, src, where).wait_send()


def exchange_scratch(vertical, side, corner):
    shapes = [vertical] * 2 + [side] * 2 + [corner] * 4
    return [pltpu.VMEM(shape, F32) for shape in shapes] + [pltpu.SemaphoreType.DMA((8,))] * 2


FIELD_SCRATCH = exchange_scratch((2, 2, HALF, SIZE), (TILE, SIZE), (HALF, SIZE))
WEIGHT_SCRATCH = exchange_scratch((2, HALF, SIZE), (TILE // 2, SIZE), (HALF, SIZE))


def as_exchange(refs):
    return Exchange(refs[:8], refs[8], refs[9])


def send_margins(exchange, own, left, right):
    lane = lanes(TILE)
    left[...] = jnp.where(lane < HALF, own[0, 0], half_turn(own[1, 0]))
    right[...] = jnp.where(lane >= HALF, own[0, 1], half_turn(own[1, 1]))
    low, high = pl.ds(0, HALF), pl.ds(TILE - HALF, HALF)
    srcs = [
        own.at[:, :, low, :], own.at[:, :, high, :], left, right,
        left.at[low], right.at[low], left.at[high], right.at[high],
    ]
    for k in (2, 3, 4, 5, 6, 7, 0, 1):
        exchange.start(k, srcs[k])
    return srcs


def fill_extended(exchange, ext):
    for k in range(8):
        exchange.wait_recv(k)
    bufs = exchange.dsts
    low, mid, high = pl.ds(0, HALF), pl.ds(HALF, TILE), pl.ds(HALF + TILE, HALF)
    ext[:, 1:3, high, :] = bufs[0][...]
    ext[:, 1:3, low, :] = bufs[1][...]
    for panel, rows, buf in (
        (3, mid, bufs[2]), (0, mid, bufs[3]),
        (3, high, bufs[4]), (0, high, bufs[5]), (3, low, bufs[6]), (0, low, bufs[7]),
    ):
        ext[0, panel, rows, :] = buf[...]
        ext[1, panel, rows, :] = half_turn(buf[...])


def send_totals(exchange, tot, left, right):
    lane = lanes(EXT)
    left[...] = jnp.where(lane >= HALF, tot[0, 0], half_turn(tot[1, 0]))
    right[...] = jnp.where(lane < HALF, tot[0, 3], half_turn(tot[1, 3]))
    low, mid, high = pl.ds(0, HALF), pl.ds(HALF, TILE), pl.ds(HALF + TILE, HALF)
    srcs = [
        tot.at[:, 1:3, low, :], tot.at[:, 1:3, high, :], left.at[mid], right.at[mid],
        left.at[low], right.at[low], left.at[high], right.at[high],
    ]
    for k in (2, 3, 4, 5, 6, 7, 0, 1):
        exchange.start(k, srcs[k])
    return srcs


def send_weights(exchange, wgt, left, right):
    lane = lanes(SIZE)
    first, second = pl.ds(HALF, SIZE), pl.ds(HALF + SIZE, SIZE)
    left[...] = jnp.where(lane >= HALF, wgt[0, first, :], half_turn(wgt[0, second, :]))
    right[...] = jnp.where(lane < HALF, wgt[3, first, :], half_turn(wgt[3, second, :]))
    low, high = pl.ds(0, HALF), pl.ds(HALF + TILE, HALF)
    srcs = [
        wgt.at[1:3, low, :], wgt.at[1:3, high, :], left, right,
        wgt.at[0, low, :], wgt.at[3, low, :], wgt.at[0, high, :], wgt.at[3, high, :],
    ]
    for k in (2, 3, 4, 5, 6, 7, 0, 1):
        exchange.start(k, srcs[k])
    return srcs


def with_corners(side, below, above):
    return jnp.concatenate(
        [side[:HALF] + above, side[HALF : TILE - HALF], side[TILE - HALF :] + below], axis=0
    )


def with_vertical(centre, below, above):
    return jnp.concatenate(
        [centre[:HALF] + above, centre[HALF : TILE - HALF], centre[TILE - HALF :] + below], axis=0
    )


def gathered_totals(exchange, tot):
    for k in range(8):
        exchange.wait_recv(k)
    bufs = exchange.dsts
    lane = lanes(TILE)
    right = with_corners(bufs[2][...], bufs[4][...], bufs[6][...])
    left = with_corners(bufs[3][...], bufs[5][...], bufs[7][...])
    rights = (right, half_turn(right))
    lefts = (left, half_turn(left))
    parts = []
    for part in range(2):
        panels = []
        for panel in range(2):
            centre = tot[part, 1 + panel, pl.ds(HALF, TILE), :]
            centre = with_vertical(centre, bufs[0][part, panel], bufs[1][part, panel])
            extra = jnp.where(lane < HALF, lefts[part], 0.0) if panel == 0 else jnp.where(lane >= HALF, rights[part], 0.0)
            panels.append(centre + extra)
        parts.append(panels)
    return parts


def gathered_weights(exchange, wgt):
    for k in range(8):
        exchange.wait_recv(k)
    bufs = exchange.dsts
    lane = lanes(TILE)
    right = jnp.concatenate([bufs[2][...], half_turn(bufs[2][...])], axis=0)
    left = jnp.concatenate([bufs[3][...], half_turn(bufs[3][...])], axis=0)
    right = with_corners(right, bufs[4][...], bufs[6][...])
    left = with_corners(left, bufs[5][...], bufs[7][...])
    panels = []
    for panel in range(2):
        centre = with_vertical(wgt[1 + panel, pl.ds(HALF, TILE), :], bufs[0][panel], bufs[1][panel])
        extra = jnp.where(lane < HALF, left, 0.0) if panel == 0 else jnp.where(lane >= HALF, right, 0.0)
        panels.append(centre + extra)
    return panels


def margins_kernel(field, ext, *refs):
    exchange, (own, left, right) = as_exchange(refs[:10]), refs[10:]
    barrier = pltpu.get_barrier_semaphore()
    count = signal_neighbours(barrier)
    exchange.clear_missing()
    for part in range(2):
        for panel in range(2):
            value = field[part, :, panel * SIZE : (panel + 1) * SIZE]
            own[part, panel] = value
            ext[part, 1 + panel, pl.ds(HALF, TILE), :] = value
    pl.semaphore_wait(barrier, count)
    srcs = send_margins(exchange, own, left, right)
    fill_extended(exchange, ext)
    for k in range(8):
        exchange.wait_send(k, srcs[k])


def middle_kernel(tot, wgt, ext, probe, new_ext, den, *refs):
    totals, weights, margins = (as_exchange(refs[i : i + 10]) for i in (0, 10, 20))
    tot_left, tot_right, wgt_left, wgt_right, own, left, right = refs[30:]
    barrier = pltpu.get_barrier_semaphore()
    count = signal_neighbours(barrier)
    for exchange in (totals, weights, margins):
        exchange.clear_missing()
    pl.semaphore_wait(barrier, count)
    tot_srcs = send_totals(totals, tot, tot_left, tot_right)
    wgt_srcs = send_weights(weights, wgt, wgt_left, wgt_right)
    power = probe[0, 0] ** 2 + probe[0, 1] ** 2 + probe[1, 0] ** 2 + probe[1, 1] ** 2
    regular = 0.1 * jnp.max(jnp.max(power, axis=0, keepdims=True), axis=1, keepdims=True) + EPSILON
    numer = gathered_totals(totals, tot)
    weight = gathered_weights(weights, wgt)
    centre = pl.ds(HALF, TILE)
    for panel in range(2):
        divisor = weight[panel] + regular
        den[panel] = divisor
        for part in range(2):
            value = (numer[part][panel] + regular * ext[part, 1 + panel, centre, :]) / divisor
            own[part, panel] = value
            new_ext[part, 1 + panel, centre, :] = value
    srcs = send_margins(margins, own, left, right)
    fill_extended(margins, new_ext)
    for k in range(8):
        totals.wait_send(k, tot_srcs[k])
        weights.wait_send(k, wgt_srcs[k])
        margins.wait_send(k, srcs[k])


SHARE = 4 * SIZE // (2 * XS * YS)


def last_kernel(tot, den, ext, probe, grad_a, grad_b, field, probe_new, *refs):
    totals = as_exchange(refs[:10])
    (tot_left, tot_right, total, from_core, half, from_plane, piece, from_line, fresh,
     core_send, core_recv, plane_send, plane_recv, line_send, line_recv,
     spread_send, spread_recv, back_send, back_recv) = refs[10:]
    row, col = lax.axis_index("row"), lax.axis_index("col")
    y, core = row // 2, row % 2
    x, z = col // ZS, col % ZS
    place = x * YS + y

    def in_plane(d):
        other = (place + d) % (XS * YS)
        return other, ((other % YS) * 2 + core, (other // YS) * ZS + z)

    def in_line(d):
        other = (z + d) % ZS
        return other, (row, x * ZS + other)

    partner = (y * 2 + (1 - core), col)
    barrier = pltpu.get_barrier_semaphore()
    count = signal_neighbours(barrier)
    pl.semaphore_signal(barrier, 1, device_id=partner, device_id_type=MESH)
    for d in range(1, XS * YS):
        pl.semaphore_signal(barrier, 1, device_id=in_plane(d)[1], device_id_type=MESH)
    for d in range(1, ZS):
        pl.semaphore_signal(barrier, 1, device_id=in_line(d)[1], device_id_type=MESH)
    totals.clear_missing()
    for part in range(2):
        for mode in range(2):
            rows = pl.ds((part * 2 + mode) * SIZE, SIZE)
            total[rows, :] = grad_a[part, mode] + grad_b[part, mode]
    pl.semaphore_wait(barrier, count + 1 + (XS * YS - 1) + (ZS - 1))

    def remote(src, dst, send, recv, where):
        return pltpu.make_async_remote_copy(src, dst, send, recv, device_id=where, device_id_type=MESH)

    middle = 2 * SIZE
    mine = pl.multiple_of(core * middle, middle)
    theirs = pl.multiple_of((1 - core) * middle, middle)
    swap = remote(total.at[pl.ds(theirs, middle)], from_core, core_send, core_recv, partner)
    swap.start()
    tot_srcs = send_totals(totals, tot, tot_left, tot_right)
    swap.wait_recv()
    half[...] = total[pl.ds(mine, middle), :] + from_core[...]

    def plane_copy(d):
        other, where = in_plane(d)
        rows = pl.ds(pl.multiple_of(other * SHARE, SHARE), SHARE)
        return remote(half.at[rows], from_plane.at[d], plane_send.at[d], plane_recv.at[d], where)

    for d in range(1, XS * YS):
        plane_copy(d).start()

    numer = gathered_totals(totals, tot)
    power = probe[0:SIZE] ** 2
    for k in range(1, 4):
        power = power + probe[k * SIZE : (k + 1) * SIZE] ** 2
    regular = 0.1 * jnp.max(jnp.max(power, axis=0, keepdims=True), axis=1, keepdims=True) + EPSILON
    for part in range(2):
        for panel in range(2):
            own = ext[part, 1 + panel, pl.ds(HALF, TILE), :]
            field[part, :, panel * SIZE : (panel + 1) * SIZE] = (numer[part][panel] + regular * own) / den[panel]

    share = half[pl.ds(pl.multiple_of(place * SHARE, SHARE), SHARE), :]
    for d in range(1, XS * YS):
        plane_copy(d).wait_recv()
        share = share + from_plane[d]
    piece[...] = share
    from_line[z] = share

    def line_copy(d):
        _, where = in_line(d)
        return remote(piece, from_line.at[z], line_send.at[d], line_recv.at[d], where)

    def line_arrival(d):
        source = (z - d + ZS) % ZS
        return remote(piece, from_line.at[source], line_send.at[d], line_recv.at[d], in_line(d)[1])

    for d in range(1, ZS):
        line_copy(d).start()
    for d in range(1, ZS):
        line_arrival(d).wait_recv()
    summed = from_line[0]
    for k in range(1, ZS):
        summed = summed + from_line[k]
    rows = pl.ds(pl.multiple_of(mine + place * SHARE, SHARE), SHARE)
    slots = float(ROWS * COLS * 24)
    fresh[rows, :] = probe[rows, :] + summed / slots

    def spread_copy(d):
        _, where = in_plane(d)
        return remote(fresh.at[rows], fresh.at[rows], spread_send.at[d], spread_recv.at[d], where)

    def spread_arrival(d):
        source = (place - d + XS * YS) % (XS * YS)
        there = pl.ds(pl.multiple_of(mine + source * SHARE, SHARE), SHARE)
        return remote(fresh.at[rows], fresh.at[there], spread_send.at[d], spread_recv.at[d], in_plane(d)[1])

    for d in range(1, XS * YS):
        spread_copy(d).start()
    for d in range(1, XS * YS):
        spread_arrival(d).wait_recv()
    back = remote(fresh.at[pl.ds(mine, middle)], fresh.at[pl.ds(mine, middle)], back_send, back_recv, partner)
    back.start()
    arrival = remote(fresh.at[pl.ds(theirs, middle)], fresh.at[pl.ds(theirs, middle)], back_send, back_recv, partner)
    arrival.wait_recv()
    probe_new[...] = fresh[...]
    swap.wait_send()
    back.wait_send()
    for d in range(1, XS * YS):
        plane_copy(d).wait_send()
        spread_copy(d).wait_send()
    for d in range(1, ZS):
        line_copy(d).wait_send()
    for k in range(8):
        totals.wait_send(k, tot_srcs[k])


def split(x):
    high = x.astype(BF16)
    return high, (x - high.astype(F32)).astype(BF16)


def dot(a, b):
    return jnp.dot(a, b, preferred_element_type=F32)


def on_rows(table, which, x):
    high, low = split(x)
    big, small = table[2 * which], table[2 * which + 1]
    return dot(big, high) + dot(big, low) + dot(small, high)


def on_columns(x, table, which):
    high, low = split(x)
    big, small = table[2 * which], table[2 * which + 1]
    return dot(high, big) + dot(low, big) + dot(high, small)


def visit_kernel(with_weight, off, cnt, ext, probe, table, amp, *refs):
    if with_weight:
        tot, wgt, grad, spread = refs
        wgt[...] = jnp.zeros_like(wgt)
    else:
        tot, grad, spread = refs
    tot[...] = jnp.zeros_like(tot)
    grad[...] = jnp.zeros_like(grad)
    spread[...] = jnp.zeros_like(spread)
    count = cnt[0]
    lane = lanes(SIZE)

    def step(index, carry):
        modes = [(probe[0, m], probe[1, m]) for m in range(2)]
        power = modes[0][0] ** 2 + modes[0][1] ** 2 + modes[1][0] ** 2 + modes[1][1] ** 2
        exits, states = [], []
        for u in range(UNROLL):
            slot = index * UNROLL + u
            row = off[slot, 0] + HALF
            col = off[slot, 1] + SIZE
            panel, shift = col // SIZE, col % SIZE
            live = (slot < count).astype(F32)
            upper = lane >= shift
            back = (SIZE - shift) % SIZE
            window = []
            for part in range(2):
                first = ext[part, panel, pl.ds(row, SIZE), :]
                second = ext[part, panel + 1, pl.ds(row, SIZE), :]
                window.append(pltpu.roll(jnp.where(upper, first, second), back, 1))
            squared = window[0] * window[0] + window[1] * window[1]
            mean = jnp.sum(jnp.sum(squared, axis=0, keepdims=True), axis=1, keepdims=True) * (1.0 / SIZE**2) + EPSILON
            scale = live / mean
            spread[...] += squared * scale
            real = jnp.concatenate([pr * window[0] - pi * window[1] for pr, pi in modes], axis=1)
            imag = jnp.concatenate([pr * window[1] + pi * window[0] for pr, pi in modes], axis=1)
            exits.append(jnp.concatenate([real, imag], axis=0))
            states.append((slot, row, panel, shift, upper, live, window[0] * scale, window[1] * scale))
        first = [on_rows(table, 1, x) for x in exits]
        turned = jnp.concatenate(
            [
                jnp.concatenate([y[:SIZE, m * SIZE : (m + 1) * SIZE], y[SIZE:, m * SIZE : (m + 1) * SIZE]], axis=1)
                for y in first
                for m in range(2)
            ],
            axis=0,
        )
        spectrum = on_columns(turned, table, 0)
        scaled = []
        for u in range(UNROLL):
            z = spectrum[u * 2 * SIZE : (u + 1) * 2 * SIZE]
            sq = z * z
            level = sq[:SIZE, :SIZE] + sq[:SIZE, SIZE:] + sq[SIZE:, :SIZE] + sq[SIZE:, SIZE:]
            factor = amp[states[u][0]] * jnp.minimum(lax.rsqrt(level), 1.0)
            both = jnp.concatenate([factor, factor], axis=1)
            scaled += [z[:SIZE] * both, z[SIZE:] * both]
        middle = on_columns(jnp.concatenate(scaled, axis=0), table, 1)
        terms = [[0.0, 0.0], [0.0, 0.0]]
        for u in range(UNROLL):
            slot, row, panel, shift, upper, live, wr, wi = states[u]
            q = middle[u * 2 * SIZE : (u + 1) * 2 * SIZE]
            revised = on_rows(
                table,
                0,
                jnp.concatenate(
                    [
                        jnp.concatenate([q[:SIZE, :SIZE], q[SIZE:, :SIZE]], axis=1),
                        jnp.concatenate([q[:SIZE, SIZE:], q[SIZE:, SIZE:]], axis=1),
                    ],
                    axis=0,
                ),
            )
            real, imag = 0.0, 0.0
            for m in range(2):
                vr = revised[:SIZE, m * SIZE : (m + 1) * SIZE]
                vi = revised[SIZE:, m * SIZE : (m + 1) * SIZE]
                pr, pi = modes[m]
                real = real + (pr * vr + pi * vi)
                imag = imag + (pr * vi - pi * vr)
                terms[m][0] = terms[m][0] + (wr * vr + wi * vi)
                terms[m][1] = terms[m][1] + (wr * vi - wi * vr)
            places = [(tot.at[0], real), (tot.at[1], imag)]
            if with_weight:
                places.append((wgt, power))
            for ref, value in places:
                moved = pltpu.roll(value * live, shift, 1)
                ref[panel, pl.ds(row, SIZE), :] += jnp.where(upper, moved, 0.0)
                ref[panel + 1, pl.ds(row, SIZE), :] += jnp.where(upper, 0.0, moved)
        for m in range(2):
            for part in range(2):
                grad[part, m] += terms[m][part]
        return carry

    lax.fori_loop(0, (count + UNROLL - 1) // UNROLL, step, 0)
    for part in range(2):
        for m in range(2):
            grad[part, m] -= probe[part, m] * spread[...]


def shape(*dims):
    return jax.ShapeDtypeStruct(dims, F32)


def visit(with_weight, off, cnt, ext, probe, table, amp):
    outs = [shape(2, 4, EXT, SIZE)] + [shape(4, EXT, SIZE)] * with_weight + [shape(2, 2, SIZE, SIZE)]
    return pl.pallas_call(
        functools.partial(visit_kernel, with_weight),
        out_shape=outs,
        in_specs=[SMEM, SMEM, VMEM, VMEM, VMEM, VMEM],
        out_specs=[VMEM] * len(outs),
        scratch_shapes=[pltpu.VMEM((SIZE, SIZE), F32)],
        compiler_params=pltpu.CompilerParams(vmem_limit_bytes=32 << 20),
        name="visit",
    )(off, cnt, ext, probe, table, amp)


def remote_call(kernel, name, collective_id, outs, scratch, *args):
    return pl.pallas_call(
        kernel,
        out_shape=outs,
        in_specs=[VMEM] * len(args),
        out_specs=jax.tree.map(lambda _: VMEM, outs),
        scratch_shapes=scratch,
        compiler_params=pltpu.CompilerParams(
            collective_id=collective_id, has_side_effects=True, vmem_limit_bytes=32 << 20
        ),
        name=name,
    )(*args)


def local(field, probe, amplitudes, offsets, counts):
    amp = amplitudes[0, 0]
    off = offsets[0, 0]
    cnt = counts[0]
    table = jnp.asarray(dft_tables())
    buffer = pltpu.VMEM((TILE, SIZE), F32)
    long = pltpu.VMEM((EXT, SIZE), F32)
    own = pltpu.VMEM((2, 2, TILE, SIZE), F32)
    ext = remote_call(
        margins_kernel, "margins", 0, shape(2, 4, EXT, SIZE), FIELD_SCRATCH + [own, buffer, buffer], field
    )
    tot, wgt, grad_a = visit(True, off, cnt, ext, probe, table, amp)
    packed = pltpu.VMEM((SIZE, SIZE), F32)
    ext, den = remote_call(
        middle_kernel, "middle", 1, [shape(2, 4, EXT, SIZE), shape(2, TILE, SIZE)],
        FIELD_SCRATCH + WEIGHT_SCRATCH + FIELD_SCRATCH + [long, long, packed, packed, own, buffer, buffer],
        tot, wgt, ext, probe,
    )
    tot, grad_b = visit(False, off, cnt, ext, probe, table, amp)
    plane, line = XS * YS, ZS
    dma = pltpu.SemaphoreType.DMA
    scratch = FIELD_SCRATCH + [
        long, long,
        pltpu.VMEM((4 * SIZE, SIZE), F32),
        pltpu.VMEM((2 * SIZE, SIZE), F32),
        pltpu.VMEM((2 * SIZE, SIZE), F32),
        pltpu.VMEM((plane, SHARE, SIZE), F32),
        pltpu.VMEM((SHARE, SIZE), F32),
        pltpu.VMEM((line, SHARE, SIZE), F32),
        pltpu.VMEM((4 * SIZE, SIZE), F32),
        dma, dma, dma((plane,)), dma((plane,)), dma((line,)), dma((line,)), dma((plane,)), dma((plane,)), dma, dma,
    ]
    field_new, probe_new = remote_call(
        last_kernel, "last", 2, [shape(2, TILE, TILE), shape(4 * SIZE, SIZE)], scratch,
        tot, den, ext, probe.reshape(4 * SIZE, SIZE), grad_a, grad_b,
    )
    return field_new, probe_new.reshape(2, 2, SIZE, SIZE)


def solution(mesh):
    in_specs = (
        P(None, "row", "col"),
        P(),
        P("row", "col", None, None, None),
        P("row", "col", None, None),
        P("row", "col"),
    )
    out_specs = (P(None, "row", "col"), P())
    return jax.shard_map(local, mesh=mesh, in_specs=in_specs, out_specs=out_specs, check_vma=False)
```

```python
import functools

import jax
import jax.numpy as jnp
import ml_dtypes
import numpy as np
from jax import lax
from jax.experimental import pallas as pl
from jax.experimental.pallas import tpu as pltpu
from jax.sharding import PartitionSpec as P

F32 = jnp.float32
BF16 = jnp.bfloat16
EPSILON = 1e-06
MESH = pl.DeviceIdType.MESH
VMEM = pl.BlockSpec(memory_space=pltpu.VMEM)
SMEM = pl.BlockSpec(memory_space=pltpu.SMEM)

SIZE = 128
TILE = 256
HALF = 64
EXT = TILE + 2 * HALF
ROWS, COLS = 8, 32
XS, YS, ZS = 4, 4, 8
PAIR = 2

DIRS = [(-1, 0), (1, 0), (0, -1), (0, 1), (-1, -1), (-1, 1), (1, -1), (1, 1)]


def dft_tables():
    k = np.arange(SIZE)
    angles = 2 * np.pi / SIZE * ((k[:, None] * k[None, :]) % SIZE)
    c, s = np.cos(angles) / np.sqrt(SIZE), np.sin(angles) / np.sqrt(SIZE)
    terms = []
    for table in (np.block([[c, -s], [s, c]]), np.block([[c, s], [-s, c]])):
        high = table.astype(ml_dtypes.bfloat16)
        low = (table - high.astype(np.float64)).astype(ml_dtypes.bfloat16)
        terms += [high, low]
    return np.stack(terms)


def half_turn(x):
    return pltpu.roll(x, HALF, 1)


def lanes(rows):
    return lax.broadcasted_iota(jnp.int32, (rows, SIZE), 1)


def neighbour(direction):
    row = lax.axis_index("row") + direction[0]
    col = lax.axis_index("col") + direction[1]
    valid = (row >= 0) & (row < ROWS) & (col >= 0) & (col < COLS)
    return (row, col), valid


def signal_neighbours(barrier):
    count = jnp.int32(0)
    for direction in DIRS:
        where, valid = neighbour(direction)

        @pl.when(valid)
        def _():
            pl.semaphore_signal(barrier, 1, device_id=where, device_id_type=MESH)

        count = count + valid.astype(jnp.int32)
    return count


class Exchange:
    def __init__(self, dsts, send, recv):
        self.dsts, self.send, self.recv = dsts, send, recv

    def copy(self, k, src, where):
        return pltpu.make_async_remote_copy(
            src, self.dsts[k], self.send.at[k], self.recv.at[k], device_id=where, device_id_type=MESH
        )

    def start(self, k, src):
        where, valid = neighbour(DIRS[k])

        @pl.when(valid)
        def _():
            self.copy(k, src, where).start()

    def clear_missing(self):
        for k, (dr, dc) in enumerate(DIRS):
            _, valid = neighbour((-dr, -dc))

            @pl.when(jnp.logical_not(valid))
            def _():
                self.dsts[k][...] = jnp.zeros_like(self.dsts[k])

    def wait_recv(self, k):
        where, valid = neighbour((-DIRS[k][0], -DIRS[k][1]))

        @pl.when(valid)
        def _():
            self.copy(k, self.dsts[k], where).wait_recv()

    def wait_send(self, k, src):
        where, valid = neighbour(DIRS[k])

        @pl.when(valid)
        def _():
            self.copy(k, src, where).wait_send()


def exchange_scratch(vertical, side, corner):
    shapes = [vertical] * 2 + [side] * 2 + [corner] * 4
    return [pltpu.VMEM(shape, F32) for shape in shapes] + [pltpu.SemaphoreType.DMA((8,))] * 2


FIELD_SCRATCH = exchange_scratch((2, 2, HALF, SIZE), (TILE, SIZE), (HALF, SIZE))
WEIGHT_SCRATCH = exchange_scratch((2, HALF, SIZE), (TILE // 2, SIZE), (HALF, SIZE))


def as_exchange(refs):
    return Exchange(refs[:8], refs[8], refs[9])


def pack_margins(own, left, right):
    lane = lanes(TILE)
    left[...] = jnp.where(lane < HALF, own[0, 0], half_turn(own[1, 0]))
    right[...] = jnp.where(lane >= HALF, own[0, 1], half_turn(own[1, 1]))


def send_margins(exchange, own, left, right):
    low, high = pl.ds(0, HALF), pl.ds(TILE - HALF, HALF)
    srcs = [
        own.at[:, :, low, :], own.at[:, :, high, :], left, right,
        left.at[low], right.at[low], left.at[high], right.at[high],
    ]
    for k in (2, 3, 4, 5, 6, 7, 0, 1):
        exchange.start(k, srcs[k])
    return srcs


def fill_extended(exchange, ext):
    for k in range(8):
        exchange.wait_recv(k)
    bufs = exchange.dsts
    low, mid, high = pl.ds(0, HALF), pl.ds(HALF, TILE), pl.ds(HALF + TILE, HALF)
    ext[:, 1:3, high, :] = bufs[0][...]
    ext[:, 1:3, low, :] = bufs[1][...]
    for panel, rows, buf in (
        (3, mid, bufs[2]), (0, mid, bufs[3]),
        (3, high, bufs[4]), (0, high, bufs[5]), (3, low, bufs[6]), (0, low, bufs[7]),
    ):
        ext[0, panel, rows, :] = buf[...]
        ext[1, panel, rows, :] = half_turn(buf[...])


def pack_totals(tot, left, right):
    lane = lanes(EXT)
    left[...] = jnp.where(lane >= HALF, tot[0, 0], half_turn(tot[1, 0]))
    right[...] = jnp.where(lane < HALF, tot[0, 3], half_turn(tot[1, 3]))


def send_totals(exchange, tot, left, right):
    low, mid, high = pl.ds(0, HALF), pl.ds(HALF, TILE), pl.ds(HALF + TILE, HALF)
    srcs = [
        tot.at[:, 1:3, low, :], tot.at[:, 1:3, high, :], left.at[mid], right.at[mid],
        left.at[low], right.at[low], left.at[high], right.at[high],
    ]
    for k in (2, 3, 4, 5, 6, 7, 0, 1):
        exchange.start(k, srcs[k])
    return srcs


def pack_weights(wgt, left, right):
    lane = lanes(SIZE)
    first, second = pl.ds(HALF, SIZE), pl.ds(HALF + SIZE, SIZE)
    left[...] = jnp.where(lane >= HALF, wgt[0, first, :], half_turn(wgt[0, second, :]))
    right[...] = jnp.where(lane < HALF, wgt[3, first, :], half_turn(wgt[3, second, :]))


def send_weights(exchange, wgt, left, right):
    low, high = pl.ds(0, HALF), pl.ds(HALF + TILE, HALF)
    srcs = [
        wgt.at[1:3, low, :], wgt.at[1:3, high, :], left, right,
        wgt.at[0, low, :], wgt.at[3, low, :], wgt.at[0, high, :], wgt.at[3, high, :],
    ]
    for k in (2, 3, 4, 5, 6, 7, 0, 1):
        exchange.start(k, srcs[k])
    return srcs


def with_corners(side, below, above):
    return jnp.concatenate(
        [side[:HALF] + above, side[HALF : TILE - HALF], side[TILE - HALF :] + below], axis=0
    )


def with_vertical(centre, below, above):
    return jnp.concatenate(
        [centre[:HALF] + above, centre[HALF : TILE - HALF], centre[TILE - HALF :] + below], axis=0
    )


def gathered_totals(exchange, tot):
    for k in range(8):
        exchange.wait_recv(k)
    bufs = exchange.dsts
    lane = lanes(TILE)
    right = with_corners(bufs[2][...], bufs[4][...], bufs[6][...])
    left = with_corners(bufs[3][...], bufs[5][...], bufs[7][...])
    rights = (right, half_turn(right))
    lefts = (left, half_turn(left))
    parts = []
    for part in range(2):
        panels = []
        for panel in range(2):
            centre = tot[part, 1 + panel, pl.ds(HALF, TILE), :]
            centre = with_vertical(centre, bufs[0][part, panel], bufs[1][part, panel])
            extra = jnp.where(lane < HALF, lefts[part], 0.0) if panel == 0 else jnp.where(lane >= HALF, rights[part], 0.0)
            panels.append(centre + extra)
        parts.append(panels)
    return parts


def gathered_weights(exchange, wgt):
    for k in range(8):
        exchange.wait_recv(k)
    bufs = exchange.dsts
    lane = lanes(TILE)
    right = jnp.concatenate([bufs[2][...], half_turn(bufs[2][...])], axis=0)
    left = jnp.concatenate([bufs[3][...], half_turn(bufs[3][...])], axis=0)
    right = with_corners(right, bufs[4][...], bufs[6][...])
    left = with_corners(left, bufs[5][...], bufs[7][...])
    panels = []
    for panel in range(2):
        centre = with_vertical(wgt[1 + panel, pl.ds(HALF, TILE), :], bufs[0][panel], bufs[1][panel])
        extra = jnp.where(lane < HALF, left, 0.0) if panel == 0 else jnp.where(lane >= HALF, right, 0.0)
        panels.append(centre + extra)
    return panels


def margins_kernel(field, ext, *refs):
    exchange, (own, left, right, arrived) = as_exchange(refs[:10]), refs[10:]
    loads = []
    for part in range(2):
        for panel in range(2):
            src = field.at[part, :, pl.ds(panel * SIZE, SIZE)]
            loads.append(pltpu.make_async_copy(src, own.at[part, panel], arrived.at[part * 2 + panel]))
            loads[-1].start()
    barrier = pltpu.get_barrier_semaphore()
    count = signal_neighbours(barrier)
    exchange.clear_missing()
    for load in loads:
        load.wait()
    pack_margins(own, left, right)
    pl.semaphore_wait(barrier, count)
    srcs = send_margins(exchange, own, left, right)
    for part in range(2):
        for panel in range(2):
            ext[part, 1 + panel, pl.ds(HALF, TILE), :] = own[part, panel]
    fill_extended(exchange, ext)
    for k in range(8):
        exchange.wait_send(k, srcs[k])


def middle_kernel(tot, wgt, ext, probe, new_ext, den, *refs):
    totals, weights, margins = (as_exchange(refs[i : i + 10]) for i in (0, 10, 20))
    tot_left, tot_right, wgt_left, wgt_right, own, left, right = refs[30:]
    barrier = pltpu.get_barrier_semaphore()
    count = signal_neighbours(barrier)
    for exchange in (totals, weights, margins):
        exchange.clear_missing()
    pack_totals(tot, tot_left, tot_right)
    pack_weights(wgt, wgt_left, wgt_right)
    pl.semaphore_wait(barrier, count)
    tot_srcs = send_totals(totals, tot, tot_left, tot_right)
    wgt_srcs = send_weights(weights, wgt, wgt_left, wgt_right)
    power = probe[0, 0] ** 2 + probe[0, 1] ** 2 + probe[1, 0] ** 2 + probe[1, 1] ** 2
    regular = 0.1 * jnp.max(jnp.max(power, axis=0, keepdims=True), axis=1, keepdims=True) + EPSILON
    numer = gathered_totals(totals, tot)
    weight = gathered_weights(weights, wgt)
    centre = pl.ds(HALF, TILE)
    for panel in range(2):
        divisor = weight[panel] + regular
        den[panel] = divisor
        for part in range(2):
            value = (numer[part][panel] + regular * ext[part, 1 + panel, centre, :]) / divisor
            own[part, panel] = value
            new_ext[part, 1 + panel, centre, :] = value
    pack_margins(own, left, right)
    srcs = send_margins(margins, own, left, right)
    fill_extended(margins, new_ext)
    for k in range(8):
        totals.wait_send(k, tot_srcs[k])
        weights.wait_send(k, wgt_srcs[k])
        margins.wait_send(k, srcs[k])


SHARE = 4 * SIZE // (2 * XS * YS)


def last_kernel(tot, den, ext, probe, grad_a, grad_b, field, probe_new, *refs):
    totals = as_exchange(refs[:10])
    (tot_left, tot_right, total, from_core, half, from_plane, piece, from_line, fresh,
     core_send, core_recv, plane_send, plane_recv, line_send, line_recv,
     spread_send, spread_recv, back_send, back_recv) = refs[10:]
    row, col = lax.axis_index("row"), lax.axis_index("col")
    y, core = row // 2, row % 2
    x, z = col // ZS, col % ZS
    place = x * YS + y

    def in_plane(d):
        other = (place + d) % (XS * YS)
        return other, ((other % YS) * 2 + core, (other // YS) * ZS + z)

    def in_line(d):
        other = (z + d) % ZS
        return other, (row, x * ZS + other)

    partner = (y * 2 + (1 - core), col)
    barrier = pltpu.get_barrier_semaphore()
    count = signal_neighbours(barrier)
    pl.semaphore_signal(barrier, 1, device_id=partner, device_id_type=MESH)
    for d in range(1, XS * YS):
        pl.semaphore_signal(barrier, 1, device_id=in_plane(d)[1], device_id_type=MESH)
    for d in range(1, ZS):
        pl.semaphore_signal(barrier, 1, device_id=in_line(d)[1], device_id_type=MESH)
    totals.clear_missing()
    for part in range(2):
        for mode in range(2):
            rows = pl.ds((part * 2 + mode) * SIZE, SIZE)
            total[rows, :] = grad_a[part, mode] + grad_b[part, mode]
    pack_totals(tot, tot_left, tot_right)
    pl.semaphore_wait(barrier, count + 1 + (XS * YS - 1) + (ZS - 1))

    def remote(src, dst, send, recv, where):
        return pltpu.make_async_remote_copy(src, dst, send, recv, device_id=where, device_id_type=MESH)

    middle = 2 * SIZE
    mine = pl.multiple_of(core * middle, middle)
    theirs = pl.multiple_of((1 - core) * middle, middle)

    def share_of(start, d):
        other, _ = in_plane(d)
        return pl.ds(pl.multiple_of(start + other * SHARE, SHARE), SHARE)

    def swap_copy(d):
        return remote(total.at[share_of(theirs, d)], from_core.at[share_of(0, d)], core_send.at[d], core_recv.at[d], partner)

    order = list(range(1, XS * YS)) + [0]
    for d in order:
        swap_copy(d).start()
    tot_srcs = send_totals(totals, tot, tot_left, tot_right)

    def plane_copy(d):
        _, where = in_plane(d)
        return remote(half.at[share_of(0, d)], from_plane.at[d], plane_send.at[d], plane_recv.at[d], where)

    for d in order:
        swap_copy(d).wait_recv()
        half[share_of(0, d), :] = total[share_of(mine, d), :] + from_core[share_of(0, d), :]
        if d:
            plane_copy(d).start()

    numer = gathered_totals(totals, tot)
    power = probe[0:SIZE] ** 2
    for k in range(1, 4):
        power = power + probe[k * SIZE : (k + 1) * SIZE] ** 2
    regular = 0.1 * jnp.max(jnp.max(power, axis=0, keepdims=True), axis=1, keepdims=True) + EPSILON
    for part in range(2):
        for panel in range(2):
            own = ext[part, 1 + panel, pl.ds(HALF, TILE), :]
            field[part, :, panel * SIZE : (panel + 1) * SIZE] = (numer[part][panel] + regular * own) / den[panel]

    share = half[pl.ds(pl.multiple_of(place * SHARE, SHARE), SHARE), :]
    for d in range(1, XS * YS):
        plane_copy(d).wait_recv()
        share = share + from_plane[d]
    piece[...] = share
    from_line[z] = share

    def line_copy(d):
        _, where = in_line(d)
        return remote(piece, from_line.at[z], line_send.at[d], line_recv.at[d], where)

    def line_arrival(d):
        source = (z - d + ZS) % ZS
        return remote(piece, from_line.at[source], line_send.at[d], line_recv.at[d], in_line(d)[1])

    for d in range(1, ZS):
        line_copy(d).start()
    for d in range(1, ZS):
        line_arrival(d).wait_recv()
    summed = from_line[0]
    for k in range(1, ZS):
        summed = summed + from_line[k]
    rows = pl.ds(pl.multiple_of(mine + place * SHARE, SHARE), SHARE)
    slots = float(ROWS * COLS * 24)
    fresh[rows, :] = probe[rows, :] + summed / slots

    def spread_copy(d):
        _, where = in_plane(d)
        return remote(fresh.at[rows], fresh.at[rows], spread_send.at[d], spread_recv.at[d], where)

    def spread_arrival(d):
        source = (place - d + XS * YS) % (XS * YS)
        there = pl.ds(pl.multiple_of(mine + source * SHARE, SHARE), SHARE)
        return remote(fresh.at[rows], fresh.at[there], spread_send.at[d], spread_recv.at[d], in_plane(d)[1])

    def back_copy(d, start):
        there = pl.ds(pl.multiple_of(start + (place - d + XS * YS) % (XS * YS) * SHARE, SHARE), SHARE)
        return remote(fresh.at[there], fresh.at[there], back_send.at[d], back_recv.at[d], partner)

    for d in range(1, XS * YS):
        spread_copy(d).start()
    back_copy(0, mine).start()
    for d in range(1, XS * YS):
        spread_arrival(d).wait_recv()
        back_copy(d, mine).start()
    for d in range(XS * YS):
        back_copy(d, theirs).wait_recv()
    probe_new[...] = fresh[...]
    for d in range(XS * YS):
        swap_copy(d).wait_send()
        back_copy(d, mine).wait_send()
    for d in range(1, XS * YS):
        plane_copy(d).wait_send()
        spread_copy(d).wait_send()
    for d in range(1, ZS):
        line_copy(d).wait_send()
    for k in range(8):
        totals.wait_send(k, tot_srcs[k])


def split(x):
    high = x.astype(BF16)
    return high, (x - high.astype(F32)).astype(BF16)


def turned(y):
    return jnp.concatenate(
        [
            jnp.concatenate([y[:SIZE, :SIZE], y[SIZE:, :SIZE]], axis=1),
            jnp.concatenate([y[:SIZE, SIZE:], y[SIZE:, SIZE:]], axis=1),
        ],
        axis=0,
    )


def visit_kernel(with_weight, *refs):
    unit = (2 * SIZE, 2 * SIZE)
    accumulators = [pltpu.ACC(u)(unit, F32) for _ in range(4) for u in range(PAIR)]
    pl.run_scoped(functools.partial(visit_slots, with_weight, refs), *accumulators)


def visit_slots(with_weight, refs, *accumulators):
    off, cnt, ext, probe, table, amp, tot, *refs = refs
    if with_weight:
        wgt, *refs = refs
        wgt[...] = jnp.zeros_like(wgt)
    grad, spread, power, *pairs, kept = refs
    exits, first, second, third = (tuple(pairs[i : i + 2]) for i in (0, 2, 4, 6))
    acc_a, acc_b, acc_c, acc_d = (accumulators[i : i + PAIR] for i in range(0, 4 * PAIR, PAIR))
    tot[...] = jnp.zeros_like(tot)
    grad[...] = jnp.zeros_like(grad)
    spread[...] = jnp.zeros_like(spread)
    if with_weight:
        power[...] = probe[0, 0] ** 2 + probe[0, 1] ** 2 + probe[1, 0] ** 2 + probe[1, 1] ** 2
    count = cnt[0, 0]
    slots = amp.shape[0]
    lane = lanes(SIZE)
    both = range(PAIR)

    def clamped(index, u):
        return jnp.minimum(index * PAIR + u, slots - 1)

    def live(index, u):
        return (index * PAIR + u < count).astype(F32)

    def corner(index, u):
        slot = clamped(index, u)
        row = off[0, slot] + HALF
        col = off[1, slot] + SIZE
        return row, col // SIZE, col % SIZE

    def on_rows(acc, which, terms, u):
        high, low = terms
        pltpu.matmul_push_rhs(high[u], 0, u)
        pltpu.matmul_push_rhs(low[u], 1, u)
        pltpu.matmul_acc_lhs(acc[u], table[2 * which], load_staged_rhs=0)
        pltpu.matmul_acc_lhs(acc[u], table[2 * which + 1])
        pltpu.matmul_acc_lhs(acc[u], table[2 * which], load_staged_rhs=1)

    def on_columns(acc, which, terms, u):
        high, low = terms
        pltpu.matmul_push_rhs(table[2 * which], 0, u)
        pltpu.matmul_push_rhs(table[2 * which + 1], 1, u)
        pltpu.matmul_acc_lhs(acc[u], high[u], load_staged_rhs=0)
        pltpu.matmul_acc_lhs(acc[u], low[u])
        pltpu.matmul_acc_lhs(acc[u], high[u], load_staged_rhs=1)

    def keep_terms(terms, u, value):
        terms[0][u], terms[1][u] = split(value)

    def fetch(index, u):
        row, panel, shift = corner(index, u)
        upper = lane >= shift
        back = (SIZE - shift) % SIZE
        window = []
        for part in range(2):
            near = ext[part, panel, pl.ds(row, SIZE), :]
            far = ext[part, panel + 1, pl.ds(row, SIZE), :]
            window.append(pltpu.roll(jnp.where(upper, near, far), back, 1))
        squared = window[0] * window[0] + window[1] * window[1]
        mean = jnp.sum(jnp.sum(squared, axis=0, keepdims=True), axis=1, keepdims=True) * (1.0 / SIZE**2) + EPSILON
        scale = live(index, u) / mean
        for m in range(2):
            pr, pi = probe[0, m], probe[1, m]
            block = pl.ds(m * SIZE, SIZE)
            for rows, value in (
                (pl.ds(0, SIZE), pr * window[0] - pi * window[1]),
                (pl.ds(SIZE, SIZE), pr * window[1] + pi * window[0]),
            ):
                high, low = split(value)
                exits[0][u, rows, block] = high
                exits[1][u, rows, block] = low
        place = index % 3
        kept[place, u, 0] = window[0] * scale
        kept[place, u, 1] = window[1] * scale
        spread[...] += squared * scale

    def rescale(index, u):
        z = pltpu.matmul_pop(acc_b[u])
        sq = z * z
        level = sq[:SIZE, :SIZE] + sq[:SIZE, SIZE:] + sq[SIZE:, :SIZE] + sq[SIZE:, SIZE:]
        factor = amp[clamped(index, u)] * (jnp.minimum(lax.rsqrt(level), 1.0) * live(index, u))
        wide = jnp.concatenate([factor, factor], axis=1)
        keep_terms(second, u, jnp.concatenate([z[:SIZE] * wide, z[SIZE:] * wide], axis=0))

    def place(index, u):
        row, panel, shift = corner(index, u)
        upper = lane >= shift
        revised = pltpu.matmul_pop(acc_d[u])
        wr, wi = kept[index % 3, u, 0], kept[index % 3, u, 1]
        real, imag, terms = 0.0, 0.0, []
        for m in range(2):
            vr = revised[:SIZE, m * SIZE : (m + 1) * SIZE]
            vi = revised[SIZE:, m * SIZE : (m + 1) * SIZE]
            pr, pi = probe[0, m], probe[1, m]
            real = real + (pr * vr + pi * vi)
            imag = imag + (pr * vi - pi * vr)
            terms.append((wr * vr + wi * vi, wr * vi - wi * vr))
        add_at(tot.at[0], row, panel, shift, upper, real)
        add_at(tot.at[1], row, panel, shift, upper, imag)
        return terms

    def add_at(ref, row, panel, shift, upper, value):
        moved = pltpu.roll(value, shift, 1)
        near, far = ref.at[panel, pl.ds(row, SIZE), :], ref.at[panel + 1, pl.ds(row, SIZE), :]
        pltpu.store(near, near[...] + moved, mask=upper)
        pltpu.store(far, far[...] + moved, mask=jnp.logical_not(upper))

    def weigh(index, u):
        if with_weight:
            row, panel, shift = corner(index, u)
            add_at(wgt, row, panel, shift, lane >= shift, power[...] * live(index, u))

    def add_terms(terms):
        for m in range(2):
            for part in range(2):
                grad[part, m] += terms[0][m][part] + terms[1][m][part]

    pairs_live = (count + PAIR - 1) // PAIR
    for u in both:
        fetch(0, u)
    for u in both:
        on_rows(acc_a, 1, exits, u)
    for u in both:
        fetch(1, u)
    for u in both:
        keep_terms(first, u, turned(pltpu.matmul_pop(acc_a[u])))
    for u in both:
        on_columns(acc_b, 0, first, u)
    for u in both:
        on_rows(acc_a, 1, exits, u)
    for u in both:
        weigh(0, u)
    for u in both:
        rescale(0, u)

    def slotwise(index, carry):
        terms = []
        for u in both:
            keep_terms(first, u, turned(pltpu.matmul_pop(acc_a[u])))
            on_columns(acc_c, 1, second, u)
            fetch(index + 1, u)
            on_columns(acc_b, 0, first, u)
            keep_terms(third, u, turned(pltpu.matmul_pop(acc_c[u])))
            on_rows(acc_d, 0, third, u)
            weigh(index, u)
            rescale(index, u)
            on_rows(acc_a, 1, exits, u)
            terms.append(place(index - 1, u))
        add_terms(terms)
        return carry

    def pairwise(index, carry):
        for u in both:
            keep_terms(first, u, turned(pltpu.matmul_pop(acc_a[u])))
        for u in both:
            on_columns(acc_c, 1, second, u)
        fetch(index + 1, 0)
        for u in both:
            keep_terms(third, u, turned(pltpu.matmul_pop(acc_c[u])))
        for u in both:
            on_columns(acc_b, 0, first, u)
        fetch(index + 1, 1)
        for u in both:
            rescale(index, u)
        for u in both:
            on_rows(acc_d, 0, third, u)
        terms = [place(index - 1, u) for u in both]
        for u in both:
            on_rows(acc_a, 1, exits, u)
        add_terms(terms)
        return carry

    lax.fori_loop(1, pairs_live, slotwise if with_weight else pairwise, 0)
    for u in both:
        on_columns(acc_c, 1, second, u)
    for u in both:
        keep_terms(third, u, turned(pltpu.matmul_pop(acc_c[u])))
    for u in both:
        on_rows(acc_d, 0, third, u)
    add_terms([place(pairs_live - 1, u) for u in both])
    for u in both:
        keep_terms(first, u, pltpu.matmul_pop(acc_a[u]))
    for part in range(2):
        for m in range(2):
            grad[part, m] -= probe[part, m] * spread[...]


def shape(*dims):
    return jax.ShapeDtypeStruct(dims, F32)


def visit(with_weight, off, cnt, ext, probe, table, amp):
    outs = [shape(2, 4, EXT, SIZE)] + [shape(4, EXT, SIZE)] * with_weight + [shape(2, 2, SIZE, SIZE)]
    return pl.pallas_call(
        functools.partial(visit_kernel, with_weight),
        out_shape=outs,
        in_specs=[SMEM, SMEM, VMEM, VMEM, VMEM, VMEM],
        out_specs=[VMEM] * len(outs),
        scratch_shapes=[pltpu.VMEM((SIZE, SIZE), F32)] * 2
        + [pltpu.VMEM((PAIR, 2 * SIZE, 2 * SIZE), BF16)] * 8
        + [pltpu.VMEM((3, PAIR, 2, SIZE, SIZE), F32)],
        compiler_params=pltpu.CompilerParams(vmem_limit_bytes=32 << 20),
        name="visit",
    )(off, cnt, ext, probe, table, amp)


def remote_call(kernel, name, collective_id, outs, scratch, *args, specs=None, cost=None):
    return pl.pallas_call(
        kernel,
        out_shape=outs,
        in_specs=specs or [VMEM] * len(args),
        out_specs=jax.tree.map(lambda _: VMEM, outs),
        scratch_shapes=scratch,
        compiler_params=pltpu.CompilerParams(
            collective_id=collective_id, has_side_effects=True, vmem_limit_bytes=32 << 20
        ),
        cost_estimate=cost,
        name=name,
    )(*args)


def local(field, probe, amplitudes, offsets, counts):
    amp = amplitudes[0, 0]
    offsets = offsets[0, 0].T
    table = jnp.asarray(dft_tables())
    buffer = pltpu.VMEM((TILE, SIZE), F32)
    long = pltpu.VMEM((EXT, SIZE), F32)
    own = pltpu.VMEM((2, 2, TILE, SIZE), F32)
    ext = remote_call(
        margins_kernel, "margins", 0, shape(2, 4, EXT, SIZE),
        FIELD_SCRATCH + [own, buffer, buffer, pltpu.SemaphoreType.DMA((4,))],
        field, specs=[pl.BlockSpec(memory_space=pltpu.HBM)], cost=pl.CostEstimate(flops=10**10, bytes_accessed=10**7, transcendentals=0),
    )
    tot, wgt, grad_a = visit(True, offsets, counts, ext, probe, table, amp)
    packed = pltpu.VMEM((SIZE, SIZE), F32)
    ext, den = remote_call(
        middle_kernel, "middle", 1, [shape(2, 4, EXT, SIZE), shape(2, TILE, SIZE)],
        FIELD_SCRATCH + WEIGHT_SCRATCH + FIELD_SCRATCH + [long, long, packed, packed, own, buffer, buffer],
        tot, wgt, ext, probe,
    )
    tot, grad_b = visit(False, offsets, counts, ext, probe, table, amp)
    plane, line = XS * YS, ZS
    dma = pltpu.SemaphoreType.DMA
    scratch = FIELD_SCRATCH + [
        long, long,
        pltpu.VMEM((4 * SIZE, SIZE), F32),
        pltpu.VMEM((2 * SIZE, SIZE), F32),
        pltpu.VMEM((2 * SIZE, SIZE), F32),
        pltpu.VMEM((plane, SHARE, SIZE), F32),
        pltpu.VMEM((SHARE, SIZE), F32),
        pltpu.VMEM((line, SHARE, SIZE), F32),
        pltpu.VMEM((4 * SIZE, SIZE), F32),
        *[dma((n,)) for n in (plane, plane, plane, plane, line, line, plane, plane, plane, plane)],
    ]
    field_new, probe_new = remote_call(
        last_kernel, "last", 2, [shape(2, TILE, TILE), shape(4 * SIZE, SIZE)], scratch,
        tot, den, ext, probe.reshape(4 * SIZE, SIZE), grad_a, grad_b,
    )
    return field_new, probe_new.reshape(2, 2, SIZE, SIZE)


def solution(mesh):
    in_specs = (
        P(None, "row", "col"),
        P(),
        P("row", "col", None, None, None),
        P("row", "col", None, None),
        P("row", "col"),
    )
    out_specs = (P(None, "row", "col"), P())
    return jax.shard_map(local, mesh=mesh, in_specs=in_specs, out_specs=out_specs, check_vma=False)
```

```python
import functools

import jax
import jax.numpy as jnp
import ml_dtypes
import numpy as np
from jax import lax
from jax.experimental import pallas as pl
from jax.experimental.pallas import tpu as pltpu
from jax.sharding import PartitionSpec as P

F32 = jnp.float32
BF16 = jnp.bfloat16
EPSILON = 1e-06
MESH = pl.DeviceIdType.MESH
VMEM = pl.BlockSpec(memory_space=pltpu.VMEM)
SMEM = pl.BlockSpec(memory_space=pltpu.SMEM)

SIZE = 128
TILE = 256
HALF = 64
EXT = TILE + 2 * HALF
ROWS, COLS = 8, 32
XS, YS, ZS = 4, 4, 8
PAIR = 2

DIRS = [(-1, 0), (1, 0), (0, -1), (0, 1), (-1, -1), (-1, 1), (1, -1), (1, 1)]


def dft_tables():
    k = np.arange(SIZE)
    angles = 2 * np.pi / SIZE * ((k[:, None] * k[None, :]) % SIZE)
    c, s = np.cos(angles) / np.sqrt(SIZE), np.sin(angles) / np.sqrt(SIZE)
    terms = []
    for table in (np.block([[c, -s], [s, c]]), np.block([[c, s], [-s, c]])):
        high = table.astype(ml_dtypes.bfloat16)
        low = (table - high.astype(np.float64)).astype(ml_dtypes.bfloat16)
        terms += [high, low]
    return np.stack(terms)


def half_turn(x):
    return pltpu.roll(x, HALF, 1)


def lanes(rows):
    return lax.broadcasted_iota(jnp.int32, (rows, SIZE), 1)


def neighbour(direction):
    row = lax.axis_index("row") + direction[0]
    col = lax.axis_index("col") + direction[1]
    valid = (row >= 0) & (row < ROWS) & (col >= 0) & (col < COLS)
    return (row, col), valid


def signal_neighbours(barrier):
    count = jnp.int32(0)
    for direction in DIRS:
        where, valid = neighbour(direction)

        @pl.when(valid)
        def _():
            pl.semaphore_signal(barrier, 1, device_id=where, device_id_type=MESH)

        count = count + valid.astype(jnp.int32)
    return count


class Exchange:
    def __init__(self, dsts, send, recv):
        self.dsts, self.send, self.recv = dsts, send, recv

    def copy(self, k, src, where):
        return pltpu.make_async_remote_copy(
            src, self.dsts[k], self.send.at[k], self.recv.at[k], device_id=where, device_id_type=MESH
        )

    def start(self, k, src):
        where, valid = neighbour(DIRS[k])

        @pl.when(valid)
        def _():
            self.copy(k, src, where).start()

    def clear_missing(self):
        for k, (dr, dc) in enumerate(DIRS):
            _, valid = neighbour((-dr, -dc))

            @pl.when(jnp.logical_not(valid))
            def _():
                self.dsts[k][...] = jnp.zeros_like(self.dsts[k])

    def wait_recv(self, k):
        where, valid = neighbour((-DIRS[k][0], -DIRS[k][1]))

        @pl.when(valid)
        def _():
            self.copy(k, self.dsts[k], where).wait_recv()

    def wait_send(self, k, src):
        where, valid = neighbour(DIRS[k])

        @pl.when(valid)
        def _():
            self.copy(k, src, where).wait_send()


def exchange_scratch(vertical, side, corner):
    shapes = [vertical] * 2 + [side] * 2 + [corner] * 4
    return [pltpu.VMEM(shape, F32) for shape in shapes] + [pltpu.SemaphoreType.DMA((8,))] * 2


FIELD_SCRATCH = exchange_scratch((2, 2, HALF, SIZE), (TILE, SIZE), (HALF, SIZE))
WEIGHT_SCRATCH = exchange_scratch((2, HALF, SIZE), (TILE // 2, SIZE), (HALF, SIZE))


def as_exchange(refs):
    return Exchange(refs[:8], refs[8], refs[9])


def pack_margins(own, left, right):
    lane = lanes(TILE)
    left[...] = jnp.where(lane < HALF, own[0, 0], half_turn(own[1, 0]))
    right[...] = jnp.where(lane >= HALF, own[0, 1], half_turn(own[1, 1]))


def send_margins(exchange, own, left, right):
    low, high = pl.ds(0, HALF), pl.ds(TILE - HALF, HALF)
    srcs = [
        own.at[:, :, low, :], own.at[:, :, high, :], left, right,
        left.at[low], right.at[low], left.at[high], right.at[high],
    ]
    for k in (2, 3, 4, 5, 6, 7, 0, 1):
        exchange.start(k, srcs[k])
    return srcs


def fill_extended(exchange, ext):
    for k in range(8):
        exchange.wait_recv(k)
    bufs = exchange.dsts
    low, mid, high = pl.ds(0, HALF), pl.ds(HALF, TILE), pl.ds(HALF + TILE, HALF)
    ext[:, 1:3, high, :] = bufs[0][...]
    ext[:, 1:3, low, :] = bufs[1][...]
    for panel, rows, buf in (
        (3, mid, bufs[2]), (0, mid, bufs[3]),
        (3, high, bufs[4]), (0, high, bufs[5]), (3, low, bufs[6]), (0, low, bufs[7]),
    ):
        ext[0, panel, rows, :] = buf[...]
        ext[1, panel, rows, :] = half_turn(buf[...])


def pack_totals(tot, left, right):
    lane = lanes(EXT)
    left[...] = jnp.where(lane >= HALF, tot[0, 0], half_turn(tot[1, 0]))
    right[...] = jnp.where(lane < HALF, tot[0, 3], half_turn(tot[1, 3]))


def send_totals(exchange, tot, left, right):
    low, mid, high = pl.ds(0, HALF), pl.ds(HALF, TILE), pl.ds(HALF + TILE, HALF)
    srcs = [
        tot.at[:, 1:3, low, :], tot.at[:, 1:3, high, :], left.at[mid], right.at[mid],
        left.at[low], right.at[low], left.at[high], right.at[high],
    ]
    for k in (2, 3, 4, 5, 6, 7, 0, 1):
        exchange.start(k, srcs[k])
    return srcs


def pack_weights(wgt, left, right):
    lane = lanes(SIZE)
    first, second = pl.ds(HALF, SIZE), pl.ds(HALF + SIZE, SIZE)
    left[...] = jnp.where(lane >= HALF, wgt[0, first, :], half_turn(wgt[0, second, :]))
    right[...] = jnp.where(lane < HALF, wgt[3, first, :], half_turn(wgt[3, second, :]))


def send_weights(exchange, wgt, left, right):
    low, high = pl.ds(0, HALF), pl.ds(HALF + TILE, HALF)
    srcs = [
        wgt.at[1:3, low, :], wgt.at[1:3, high, :], left, right,
        wgt.at[0, low, :], wgt.at[3, low, :], wgt.at[0, high, :], wgt.at[3, high, :],
    ]
    for k in (2, 3, 4, 5, 6, 7, 0, 1):
        exchange.start(k, srcs[k])
    return srcs


def with_corners(side, below, above):
    return jnp.concatenate(
        [side[:HALF] + above, side[HALF : TILE - HALF], side[TILE - HALF :] + below], axis=0
    )


def with_vertical(centre, below, above):
    return jnp.concatenate(
        [centre[:HALF] + above, centre[HALF : TILE - HALF], centre[TILE - HALF :] + below], axis=0
    )


def gathered_totals(exchange, tot):
    for k in range(8):
        exchange.wait_recv(k)
    bufs = exchange.dsts
    lane = lanes(TILE)
    right = with_corners(bufs[2][...], bufs[4][...], bufs[6][...])
    left = with_corners(bufs[3][...], bufs[5][...], bufs[7][...])
    rights = (right, half_turn(right))
    lefts = (left, half_turn(left))
    parts = []
    for part in range(2):
        panels = []
        for panel in range(2):
            centre = tot[part, 1 + panel, pl.ds(HALF, TILE), :]
            centre = with_vertical(centre, bufs[0][part, panel], bufs[1][part, panel])
            extra = jnp.where(lane < HALF, lefts[part], 0.0) if panel == 0 else jnp.where(lane >= HALF, rights[part], 0.0)
            panels.append(centre + extra)
        parts.append(panels)
    return parts


def gathered_weights(exchange, wgt):
    for k in range(8):
        exchange.wait_recv(k)
    bufs = exchange.dsts
    lane = lanes(TILE)
    right = jnp.concatenate([bufs[2][...], half_turn(bufs[2][...])], axis=0)
    left = jnp.concatenate([bufs[3][...], half_turn(bufs[3][...])], axis=0)
    right = with_corners(right, bufs[4][...], bufs[6][...])
    left = with_corners(left, bufs[5][...], bufs[7][...])
    panels = []
    for panel in range(2):
        centre = with_vertical(wgt[1 + panel, pl.ds(HALF, TILE), :], bufs[0][panel], bufs[1][panel])
        extra = jnp.where(lane < HALF, left, 0.0) if panel == 0 else jnp.where(lane >= HALF, right, 0.0)
        panels.append(centre + extra)
    return panels


def margins_kernel(field, ext, *refs):
    exchange, (own, left, right, arrived) = as_exchange(refs[:10]), refs[10:]
    loads = []
    for part in range(2):
        for panel in range(2):
            src = field.at[part, :, pl.ds(panel * SIZE, SIZE)]
            loads.append(pltpu.make_async_copy(src, own.at[part, panel], arrived.at[part * 2 + panel]))
            loads[-1].start()
    barrier = pltpu.get_barrier_semaphore()
    count = signal_neighbours(barrier)
    exchange.clear_missing()
    for load in loads:
        load.wait()
    pack_margins(own, left, right)
    pl.semaphore_wait(barrier, count)
    srcs = send_margins(exchange, own, left, right)
    for part in range(2):
        for panel in range(2):
            ext[part, 1 + panel, pl.ds(HALF, TILE), :] = own[part, panel]
    fill_extended(exchange, ext)
    for k in range(8):
        exchange.wait_send(k, srcs[k])


def middle_kernel(tot, wgt, ext, probe, new_ext, den, *refs):
    totals, weights, margins = (as_exchange(refs[i : i + 10]) for i in (0, 10, 20))
    tot_left, tot_right, wgt_left, wgt_right, own, left, right = refs[30:]
    barrier = pltpu.get_barrier_semaphore()
    count = signal_neighbours(barrier)
    for exchange in (totals, weights, margins):
        exchange.clear_missing()
    pack_totals(tot, tot_left, tot_right)
    pack_weights(wgt, wgt_left, wgt_right)
    pl.semaphore_wait(barrier, count)
    tot_srcs = send_totals(totals, tot, tot_left, tot_right)
    wgt_srcs = send_weights(weights, wgt, wgt_left, wgt_right)
    power = probe[0, 0] ** 2 + probe[0, 1] ** 2 + probe[1, 0] ** 2 + probe[1, 1] ** 2
    regular = 0.1 * jnp.max(jnp.max(power, axis=0, keepdims=True), axis=1, keepdims=True) + EPSILON
    numer = gathered_totals(totals, tot)
    weight = gathered_weights(weights, wgt)
    centre = pl.ds(HALF, TILE)
    for panel in range(2):
        divisor = weight[panel] + regular
        den[panel] = divisor
        for part in range(2):
            value = (numer[part][panel] + regular * ext[part, 1 + panel, centre, :]) / divisor
            own[part, panel] = value
            new_ext[part, 1 + panel, centre, :] = value
    pack_margins(own, left, right)
    srcs = send_margins(margins, own, left, right)
    fill_extended(margins, new_ext)
    for k in range(8):
        totals.wait_send(k, tot_srcs[k])
        weights.wait_send(k, wgt_srcs[k])
        margins.wait_send(k, srcs[k])


FAR_FIRST = sorted(
    range(XS * YS), key=lambda d: -(min(d // YS, XS - d // YS) + min(d % YS, YS - d % YS))
)
SHARE = 4 * SIZE // (2 * XS * YS)


def last_kernel(tot, den, ext, probe, grad_a, grad_b, field, probe_new, *refs):
    totals = as_exchange(refs[:10])
    (tot_left, tot_right, total, from_core, half, from_plane, piece, from_line, fresh,
     core_send, core_recv, plane_send, plane_recv, line_send, line_recv,
     spread_send, spread_recv, back_send, back_recv) = refs[10:]
    row, col = lax.axis_index("row"), lax.axis_index("col")
    y, core = row // 2, row % 2
    x, z = col // ZS, col % ZS
    place = x * YS + y

    def plane_place(step_x, step_y):
        return (x + step_x + XS) % XS * YS + (y + step_y + YS) % YS

    def in_plane(d):
        other = plane_place(d // YS, d % YS)
        return other, ((other % YS) * 2 + core, (other // YS) * ZS + z)

    def source_in_plane(d):
        return plane_place(-(d // YS), -(d % YS))

    def in_line(d):
        other = (z + d) % ZS
        return other, (row, x * ZS + other)

    partner = (y * 2 + (1 - core), col)
    barrier = pltpu.get_barrier_semaphore()
    count = signal_neighbours(barrier)
    pl.semaphore_signal(barrier, 1, device_id=partner, device_id_type=MESH)
    for d in range(1, XS * YS):
        pl.semaphore_signal(barrier, 1, device_id=in_plane(d)[1], device_id_type=MESH)
    for d in range(1, ZS):
        pl.semaphore_signal(barrier, 1, device_id=in_line(d)[1], device_id_type=MESH)
    totals.clear_missing()
    for part in range(2):
        for mode in range(2):
            rows = pl.ds((part * 2 + mode) * SIZE, SIZE)
            total[rows, :] = grad_a[part, mode] + grad_b[part, mode]
    pack_totals(tot, tot_left, tot_right)
    pl.semaphore_wait(barrier, count + 1 + (XS * YS - 1) + (ZS - 1))

    def remote(src, dst, send, recv, where):
        return pltpu.make_async_remote_copy(src, dst, send, recv, device_id=where, device_id_type=MESH)

    middle = 2 * SIZE
    mine = pl.multiple_of(core * middle, middle)
    theirs = pl.multiple_of((1 - core) * middle, middle)

    def share_of(start, d):
        other, _ = in_plane(d)
        return pl.ds(pl.multiple_of(start + other * SHARE, SHARE), SHARE)

    def swap_copy(d):
        return remote(total.at[share_of(theirs, d)], from_core.at[share_of(0, d)], core_send.at[d], core_recv.at[d], partner)

    for d in FAR_FIRST:
        swap_copy(d).start()
    tot_srcs = send_totals(totals, tot, tot_left, tot_right)

    def plane_copy(d):
        _, where = in_plane(d)
        return remote(half.at[share_of(0, d)], from_plane.at[d], plane_send.at[d], plane_recv.at[d], where)

    for d in FAR_FIRST:
        swap_copy(d).wait_recv()
        half[share_of(0, d), :] = total[share_of(mine, d), :] + from_core[share_of(0, d), :]
        if d:
            plane_copy(d).start()

    share = half[pl.ds(pl.multiple_of(place * SHARE, SHARE), SHARE), :]
    for d in FAR_FIRST[-2::-1]:
        plane_copy(d).wait_recv()
        share = share + from_plane[d]
    piece[...] = share
    from_line[z] = share

    def line_copy(d):
        _, where = in_line(d)
        return remote(piece, from_line.at[z], line_send.at[d], line_recv.at[d], where)

    def line_arrival(d):
        source = (z - d + ZS) % ZS
        return remote(piece, from_line.at[source], line_send.at[d], line_recv.at[d], in_line(d)[1])

    for d in range(1, ZS):
        line_copy(d).start()
    numer = gathered_totals(totals, tot)
    power = probe[0:SIZE] ** 2
    for k in range(1, 4):
        power = power + probe[k * SIZE : (k + 1) * SIZE] ** 2
    regular = 0.1 * jnp.max(jnp.max(power, axis=0, keepdims=True), axis=1, keepdims=True) + EPSILON
    for part in range(2):
        for panel in range(2):
            own = ext[part, 1 + panel, pl.ds(HALF, TILE), :]
            field[part, :, panel * SIZE : (panel + 1) * SIZE] = (numer[part][panel] + regular * own) / den[panel]
    for d in range(1, ZS):
        line_arrival(d).wait_recv()
    summed = from_line[0]
    for k in range(1, ZS):
        summed = summed + from_line[k]
    rows = pl.ds(pl.multiple_of(mine + place * SHARE, SHARE), SHARE)
    slots = float(ROWS * COLS * 24)
    fresh[rows, :] = probe[rows, :] + summed / slots

    def spread_copy(d):
        _, where = in_plane(d)
        return remote(fresh.at[rows], fresh.at[rows], spread_send.at[d], spread_recv.at[d], where)

    def spread_arrival(d):
        there = pl.ds(pl.multiple_of(mine + source_in_plane(d) * SHARE, SHARE), SHARE)
        return remote(fresh.at[rows], fresh.at[there], spread_send.at[d], spread_recv.at[d], in_plane(d)[1])

    def back_copy(d, start):
        there = pl.ds(pl.multiple_of(start + source_in_plane(d) * SHARE, SHARE), SHARE)
        return remote(fresh.at[there], fresh.at[there], back_send.at[d], back_recv.at[d], partner)

    for d in FAR_FIRST[:-1]:
        spread_copy(d).start()
    back_copy(0, mine).start()
    for d in FAR_FIRST[-2::-1]:
        spread_arrival(d).wait_recv()
        back_copy(d, mine).start()
    for d in range(XS * YS):
        back_copy(d, theirs).wait_recv()
    probe_new[...] = fresh[...]
    for d in range(XS * YS):
        swap_copy(d).wait_send()
        back_copy(d, mine).wait_send()
    for d in range(1, XS * YS):
        plane_copy(d).wait_send()
        spread_copy(d).wait_send()
    for d in range(1, ZS):
        line_copy(d).wait_send()
    for k in range(8):
        totals.wait_send(k, tot_srcs[k])


def split(x):
    high = x.astype(BF16)
    return high, (x - high.astype(F32)).astype(BF16)


def turned(y):
    return jnp.concatenate(
        [
            jnp.concatenate([y[:SIZE, :SIZE], y[SIZE:, :SIZE]], axis=1),
            jnp.concatenate([y[:SIZE, SIZE:], y[SIZE:, SIZE:]], axis=1),
        ],
        axis=0,
    )


def visit_kernel(with_weight, *refs):
    unit = (2 * SIZE, 2 * SIZE)
    accumulators = [pltpu.ACC(u)(unit, F32) for _ in range(4) for u in range(PAIR)]
    pl.run_scoped(functools.partial(visit_slots, with_weight, refs), *accumulators)


def visit_slots(with_weight, refs, *accumulators):
    off, cnt, ext, probe, table, amp, tot, *refs = refs
    if with_weight:
        wgt, *refs = refs
        wgt[...] = jnp.zeros_like(wgt)
    grad, spread, power, *pairs, kept = refs
    exits, first, second, third = (tuple(pairs[i : i + 2]) for i in (0, 2, 4, 6))
    acc_a, acc_b, acc_c, acc_d = (accumulators[i : i + PAIR] for i in range(0, 4 * PAIR, PAIR))
    tot[...] = jnp.zeros_like(tot)
    grad[...] = jnp.zeros_like(grad)
    spread[...] = jnp.zeros_like(spread)
    if with_weight:
        power[...] = probe[0, 0] ** 2 + probe[0, 1] ** 2 + probe[1, 0] ** 2 + probe[1, 1] ** 2
    count = cnt[0, 0]
    slots = amp.shape[0]
    lane = lanes(SIZE)
    both = range(PAIR)

    def clamped(index, u):
        return jnp.minimum(index * PAIR + u, slots - 1)

    def live(index, u):
        return (index * PAIR + u < count).astype(F32)

    def corner(index, u):
        slot = clamped(index, u)
        row = off[0, slot] + HALF
        col = off[1, slot] + SIZE
        return row, col // SIZE, col % SIZE

    def on_rows(acc, which, terms, u):
        high, low = terms
        pltpu.matmul_push_rhs(high[u], 0, u)
        pltpu.matmul_push_rhs(low[u], 1, u)
        pltpu.matmul_acc_lhs(acc[u], table[2 * which], load_staged_rhs=0)
        pltpu.matmul_acc_lhs(acc[u], table[2 * which + 1])
        pltpu.matmul_acc_lhs(acc[u], table[2 * which], load_staged_rhs=1)

    def on_columns(acc, which, terms, u):
        high, low = terms
        pltpu.matmul_push_rhs(table[2 * which], 0, u)
        pltpu.matmul_push_rhs(table[2 * which + 1], 1, u)
        pltpu.matmul_acc_lhs(acc[u], high[u], load_staged_rhs=0)
        pltpu.matmul_acc_lhs(acc[u], low[u])
        pltpu.matmul_acc_lhs(acc[u], high[u], load_staged_rhs=1)

    def keep_terms(terms, u, value):
        terms[0][u], terms[1][u] = split(value)

    def fetch(index, u):
        row, panel, shift = corner(index, u)
        upper = lane >= shift
        back = (SIZE - shift) % SIZE
        window = []
        for part in range(2):
            near = ext[part, panel, pl.ds(row, SIZE), :]
            far = ext[part, panel + 1, pl.ds(row, SIZE), :]
            window.append(pltpu.roll(jnp.where(upper, near, far), back, 1))
        squared = window[0] * window[0] + window[1] * window[1]
        mean = jnp.sum(jnp.sum(squared, axis=0, keepdims=True), axis=1, keepdims=True) * (1.0 / SIZE**2) + EPSILON
        scale = live(index, u) / mean
        for m in range(2):
            pr, pi = probe[0, m], probe[1, m]
            block = pl.ds(m * SIZE, SIZE)
            for rows, value in (
                (pl.ds(0, SIZE), pr * window[0] - pi * window[1]),
                (pl.ds(SIZE, SIZE), pr * window[1] + pi * window[0]),
            ):
                high, low = split(value)
                exits[0][u, rows, block] = high
                exits[1][u, rows, block] = low
        place = index % 3
        kept[place, u, 0] = window[0] * scale
        kept[place, u, 1] = window[1] * scale
        spread[...] += squared * scale

    def rescale(index, u):
        z = pltpu.matmul_pop(acc_b[u])
        sq = z * z
        level = sq[:SIZE, :SIZE] + sq[:SIZE, SIZE:] + sq[SIZE:, :SIZE] + sq[SIZE:, SIZE:]
        factor = amp[clamped(index, u)] * (jnp.minimum(lax.rsqrt(level), 1.0) * live(index, u))
        wide = jnp.concatenate([factor, factor], axis=1)
        keep_terms(second, u, jnp.concatenate([z[:SIZE] * wide, z[SIZE:] * wide], axis=0))

    def place(index, u):
        row, panel, shift = corner(index, u)
        upper = lane >= shift
        revised = pltpu.matmul_pop(acc_d[u])
        wr, wi = kept[index % 3, u, 0], kept[index % 3, u, 1]
        real, imag, terms = 0.0, 0.0, []
        for m in range(2):
            vr = revised[:SIZE, m * SIZE : (m + 1) * SIZE]
            vi = revised[SIZE:, m * SIZE : (m + 1) * SIZE]
            pr, pi = probe[0, m], probe[1, m]
            real = real + (pr * vr + pi * vi)
            imag = imag + (pr * vi - pi * vr)
            terms.append((wr * vr + wi * vi, wr * vi - wi * vr))
        add_at(tot.at[0], row, panel, shift, upper, real)
        add_at(tot.at[1], row, panel, shift, upper, imag)
        return terms

    def add_at(ref, row, panel, shift, upper, value):
        moved = pltpu.roll(value, shift, 1)
        near, far = ref.at[panel, pl.ds(row, SIZE), :], ref.at[panel + 1, pl.ds(row, SIZE), :]
        pltpu.store(near, near[...] + moved, mask=upper)
        pltpu.store(far, far[...] + moved, mask=jnp.logical_not(upper))

    def weigh(index, u):
        if with_weight:
            row, panel, shift = corner(index, u)
            add_at(wgt, row, panel, shift, lane >= shift, power[...] * live(index, u))

    def add_terms(terms):
        for m in range(2):
            for part in range(2):
                grad[part, m] += terms[0][m][part] + terms[1][m][part]

    pairs_live = (count + PAIR - 1) // PAIR
    for u in both:
        fetch(0, u)
    for u in both:
        on_rows(acc_a, 1, exits, u)
    for u in both:
        fetch(1, u)
    for u in both:
        keep_terms(first, u, turned(pltpu.matmul_pop(acc_a[u])))
    for u in both:
        on_columns(acc_b, 0, first, u)
    for u in both:
        on_rows(acc_a, 1, exits, u)
    for u in both:
        weigh(0, u)
    for u in both:
        rescale(0, u)

    def slotwise(index, carry):
        terms = []
        for u in both:
            keep_terms(first, u, turned(pltpu.matmul_pop(acc_a[u])))
            on_columns(acc_c, 1, second, u)
            fetch(index + 1, u)
            on_columns(acc_b, 0, first, u)
            keep_terms(third, u, turned(pltpu.matmul_pop(acc_c[u])))
            on_rows(acc_d, 0, third, u)
            weigh(index, u)
            rescale(index, u)
            on_rows(acc_a, 1, exits, u)
            terms.append(place(index - 1, u))
        add_terms(terms)
        return carry

    def pairwise(index, carry):
        for u in both:
            keep_terms(first, u, turned(pltpu.matmul_pop(acc_a[u])))
        for u in both:
            on_columns(acc_c, 1, second, u)
        fetch(index + 1, 0)
        for u in both:
            keep_terms(third, u, turned(pltpu.matmul_pop(acc_c[u])))
        for u in both:
            on_columns(acc_b, 0, first, u)
        fetch(index + 1, 1)
        for u in both:
            rescale(index, u)
        for u in both:
            on_rows(acc_d, 0, third, u)
        terms = [place(index - 1, u) for u in both]
        for u in both:
            on_rows(acc_a, 1, exits, u)
        add_terms(terms)
        return carry

    lax.fori_loop(1, pairs_live, slotwise if with_weight else pairwise, 0)
    for u in both:
        on_columns(acc_c, 1, second, u)
    for u in both:
        keep_terms(third, u, turned(pltpu.matmul_pop(acc_c[u])))
    for u in both:
        on_rows(acc_d, 0, third, u)
    add_terms([place(pairs_live - 1, u) for u in both])
    for u in both:
        keep_terms(first, u, pltpu.matmul_pop(acc_a[u]))
    for part in range(2):
        for m in range(2):
            grad[part, m] -= probe[part, m] * spread[...]


def store_kernel(field, probe, field_out, probe_out, done):
    copies = [
        pltpu.make_async_copy(field.at[0], field_out.at[0], done.at[0]),
        pltpu.make_async_copy(field.at[1], field_out.at[1], done.at[1]),
        pltpu.make_async_copy(probe, probe_out, done.at[2]),
    ]
    for copy in copies:
        copy.start()
    for copy in copies:
        copy.wait()


def store(field, probe):
    hbm = pl.BlockSpec(memory_space=pltpu.HBM)
    return pl.pallas_call(
        store_kernel,
        out_shape=[shape(*field.shape), shape(*probe.shape)],
        in_specs=[VMEM, VMEM],
        out_specs=[hbm, hbm],
        scratch_shapes=[pltpu.SemaphoreType.DMA((3,))],
        compiler_params=pltpu.CompilerParams(vmem_limit_bytes=32 << 20),
        name="store",
    )(field, probe)


def shape(*dims):
    return jax.ShapeDtypeStruct(dims, F32)


def visit(with_weight, off, cnt, ext, probe, table, amp):
    outs = [shape(2, 4, EXT, SIZE)] + [shape(4, EXT, SIZE)] * with_weight + [shape(2, 2, SIZE, SIZE)]
    return pl.pallas_call(
        functools.partial(visit_kernel, with_weight),
        out_shape=outs,
        in_specs=[SMEM, SMEM, VMEM, VMEM, VMEM, VMEM],
        out_specs=[VMEM] * len(outs),
        scratch_shapes=[pltpu.VMEM((SIZE, SIZE), F32)] * 2
        + [pltpu.VMEM((PAIR, 2 * SIZE, 2 * SIZE), BF16)] * 8
        + [pltpu.VMEM((3, PAIR, 2, SIZE, SIZE), F32)],
        compiler_params=pltpu.CompilerParams(vmem_limit_bytes=32 << 20),
        name="visit",
    )(off, cnt, ext, probe, table, amp)


def remote_call(kernel, name, collective_id, outs, scratch, *args, specs=None, cost=None):
    return pl.pallas_call(
        kernel,
        out_shape=outs,
        in_specs=specs or [VMEM] * len(args),
        out_specs=jax.tree.map(lambda _: VMEM, outs),
        scratch_shapes=scratch,
        compiler_params=pltpu.CompilerParams(
            collective_id=collective_id, has_side_effects=True, vmem_limit_bytes=32 << 20
        ),
        cost_estimate=cost,
        name=name,
    )(*args)


def local(field, probe, amplitudes, offsets, counts):
    amp = amplitudes[0, 0]
    offsets = offsets[0, 0].T
    table = jnp.asarray(dft_tables())
    buffer = pltpu.VMEM((TILE, SIZE), F32)
    long = pltpu.VMEM((EXT, SIZE), F32)
    own = pltpu.VMEM((2, 2, TILE, SIZE), F32)
    ext = remote_call(
        margins_kernel, "margins", 0, shape(2, 4, EXT, SIZE),
        FIELD_SCRATCH + [own, buffer, buffer, pltpu.SemaphoreType.DMA((4,))],
        pltpu.with_memory_space_constraint(field, pltpu.HBM), specs=[pl.BlockSpec(memory_space=pltpu.HBM)], cost=pl.CostEstimate(flops=10**10, bytes_accessed=10**7, transcendentals=0),
    )
    tot, wgt, grad_a = visit(True, offsets, counts, ext, probe, table, amp)
    packed = pltpu.VMEM((SIZE, SIZE), F32)
    ext, den = remote_call(
        middle_kernel, "middle", 1, [shape(2, 4, EXT, SIZE), shape(2, TILE, SIZE)],
        FIELD_SCRATCH + WEIGHT_SCRATCH + FIELD_SCRATCH + [long, long, packed, packed, own, buffer, buffer],
        tot, wgt, ext, probe,
    )
    tot, grad_b = visit(False, offsets, counts, ext, probe, table, amp)
    plane, line = XS * YS, ZS
    dma = pltpu.SemaphoreType.DMA
    scratch = FIELD_SCRATCH + [
        long, long,
        pltpu.VMEM((4 * SIZE, SIZE), F32),
        pltpu.VMEM((2 * SIZE, SIZE), F32),
        pltpu.VMEM((2 * SIZE, SIZE), F32),
        pltpu.VMEM((plane, SHARE, SIZE), F32),
        pltpu.VMEM((SHARE, SIZE), F32),
        pltpu.VMEM((line, SHARE, SIZE), F32),
        pltpu.VMEM((4 * SIZE, SIZE), F32),
        *[dma((n,)) for n in (plane, plane, plane, plane, line, line, plane, plane, plane, plane)],
    ]
    field_new, probe_new = remote_call(
        last_kernel, "last", 2, [shape(2, TILE, TILE), shape(4 * SIZE, SIZE)], scratch,
        tot, den, ext, probe.reshape(4 * SIZE, SIZE), grad_a, grad_b,
    )
    return store(field_new, probe_new.reshape(2, 2, SIZE, SIZE))


def solution(mesh):
    in_specs = (
        P(None, "row", "col"),
        P(),
        P("row", "col", None, None, None),
        P("row", "col", None, None),
        P("row", "col"),
    )
    out_specs = (P(None, "row", "col"), P())
    return jax.shard_map(local, mesh=mesh, in_specs=in_specs, out_specs=out_specs, check_vma=False)
```

```python
import functools

import jax
import jax.numpy as jnp
import ml_dtypes
import numpy as np
from jax import lax
from jax.experimental import pallas as pl
from jax.experimental.pallas import tpu as pltpu
from jax.sharding import PartitionSpec as P

F32 = jnp.float32
BF16 = jnp.bfloat16
EPSILON = 1e-06
MESH = pl.DeviceIdType.MESH
VMEM = pl.BlockSpec(memory_space=pltpu.VMEM)
SMEM = pl.BlockSpec(memory_space=pltpu.SMEM)

SIZE = 128
TILE = 256
HALF = 64
EXT = TILE + 2 * HALF
ROWS, COLS = 8, 32
XS, YS, ZS = 4, 4, 8
PAIR = 2

DIRS = [(-1, 0), (1, 0), (0, -1), (0, 1), (-1, -1), (-1, 1), (1, -1), (1, 1)]
SEND_ORDER = (4, 5, 6, 7, 2, 3, 0, 1)


def dft_tables():
    k = np.arange(SIZE)
    angles = 2 * np.pi / SIZE * ((k[:, None] * k[None, :]) % SIZE)
    c, s = np.cos(angles) / np.sqrt(SIZE), np.sin(angles) / np.sqrt(SIZE)
    terms = []
    for table in (np.block([[c, -s], [s, c]]), np.block([[c, s], [-s, c]])):
        high = table.astype(ml_dtypes.bfloat16)
        low = (table - high.astype(np.float64)).astype(ml_dtypes.bfloat16)
        terms += [high, low]
    return np.stack(terms)


def half_turn(x):
    return pltpu.roll(x, HALF, 1)


def lanes(rows):
    return lax.broadcasted_iota(jnp.int32, (rows, SIZE), 1)


def neighbour(direction):
    row = lax.axis_index("row") + direction[0]
    col = lax.axis_index("col") + direction[1]
    valid = (row >= 0) & (row < ROWS) & (col >= 0) & (col < COLS)
    return (row, col), valid


def signal_neighbours(barrier):
    count = jnp.int32(0)
    for direction in DIRS:
        where, valid = neighbour(direction)

        @pl.when(valid)
        def _():
            pl.semaphore_signal(barrier, 1, device_id=where, device_id_type=MESH)

        count = count + valid.astype(jnp.int32)
    return count


class Exchange:
    def __init__(self, dsts, send, recv):
        self.dsts, self.send, self.recv = dsts, send, recv

    def copy(self, k, src, where):
        return pltpu.make_async_remote_copy(
            src, self.dsts[k], self.send.at[k], self.recv.at[k], device_id=where, device_id_type=MESH
        )

    def start(self, k, src):
        where, valid = neighbour(DIRS[k])

        @pl.when(valid)
        def _():
            self.copy(k, src, where).start()

    def clear_missing(self):
        for k, (dr, dc) in enumerate(DIRS):
            _, valid = neighbour((-dr, -dc))

            @pl.when(jnp.logical_not(valid))
            def _():
                self.dsts[k][...] = jnp.zeros_like(self.dsts[k])

    def wait_recv(self, k):
        where, valid = neighbour((-DIRS[k][0], -DIRS[k][1]))

        @pl.when(valid)
        def _():
            self.copy(k, self.dsts[k], where).wait_recv()

    def wait_send(self, k, src):
        where, valid = neighbour(DIRS[k])

        @pl.when(valid)
        def _():
            self.copy(k, src, where).wait_send()


def exchange_scratch(vertical, side, corner):
    shapes = [vertical] * 2 + [side] * 2 + [corner] * 4
    return [pltpu.VMEM(shape, F32) for shape in shapes] + [pltpu.SemaphoreType.DMA((8,))] * 2


FIELD_SCRATCH = exchange_scratch((2, 2, HALF, SIZE), (TILE, SIZE), (HALF, SIZE))
WEIGHT_SCRATCH = exchange_scratch((2, HALF, SIZE), (TILE // 2, SIZE), (HALF, SIZE))


def as_exchange(refs):
    return Exchange(refs[:8], refs[8], refs[9])


def pack_margins(own, left, right):
    lane = lanes(TILE)
    left[...] = jnp.where(lane < HALF, own[0, 0], half_turn(own[1, 0]))
    right[...] = jnp.where(lane >= HALF, own[0, 1], half_turn(own[1, 1]))


def send_margins(exchange, own, left, right):
    low, high = pl.ds(0, HALF), pl.ds(TILE - HALF, HALF)
    srcs = [
        own.at[:, :, low, :], own.at[:, :, high, :], left, right,
        left.at[low], right.at[low], left.at[high], right.at[high],
    ]
    for k in SEND_ORDER:
        exchange.start(k, srcs[k])
    return srcs


def fill_extended(exchange, ext):
    bufs = exchange.dsts
    low, mid, high = pl.ds(0, HALF), pl.ds(HALF, TILE), pl.ds(HALF + TILE, HALF)
    for k, rows in ((0, high), (1, low)):
        exchange.wait_recv(k)
        ext[:, 1:3, rows, :] = bufs[k][...]
    for k, panel, rows in ((4, 3, high), (5, 0, high), (6, 3, low), (7, 0, low), (2, 3, mid), (3, 0, mid)):
        exchange.wait_recv(k)
        ext[0, panel, rows, :] = bufs[k][...]
        ext[1, panel, rows, :] = half_turn(bufs[k][...])


def pack_totals(tot, left, right):
    lane = lanes(EXT)
    left[...] = jnp.where(lane >= HALF, tot[0, 0], half_turn(tot[1, 0]))
    right[...] = jnp.where(lane < HALF, tot[0, 3], half_turn(tot[1, 3]))


def send_totals(exchange, tot, left, right):
    low, mid, high = pl.ds(0, HALF), pl.ds(HALF, TILE), pl.ds(HALF + TILE, HALF)
    srcs = [
        tot.at[:, 1:3, low, :], tot.at[:, 1:3, high, :], left.at[mid], right.at[mid],
        left.at[low], right.at[low], left.at[high], right.at[high],
    ]
    for k in SEND_ORDER:
        exchange.start(k, srcs[k])
    return srcs


def pack_weights(wgt, left, right):
    lane = lanes(SIZE)
    first, second = pl.ds(HALF, SIZE), pl.ds(HALF + SIZE, SIZE)
    left[...] = jnp.where(lane >= HALF, wgt[0, first, :], half_turn(wgt[0, second, :]))
    right[...] = jnp.where(lane < HALF, wgt[3, first, :], half_turn(wgt[3, second, :]))


def send_weights(exchange, wgt, left, right):
    low, high = pl.ds(0, HALF), pl.ds(HALF + TILE, HALF)
    srcs = [
        wgt.at[1:3, low, :], wgt.at[1:3, high, :], left, right,
        wgt.at[0, low, :], wgt.at[3, low, :], wgt.at[0, high, :], wgt.at[3, high, :],
    ]
    for k in SEND_ORDER:
        exchange.start(k, srcs[k])
    return srcs


def with_corners(side, below, above):
    return jnp.concatenate(
        [side[:HALF] + above, side[HALF : TILE - HALF], side[TILE - HALF :] + below], axis=0
    )


def with_vertical(centre, below, above):
    return jnp.concatenate(
        [centre[:HALF] + above, centre[HALF : TILE - HALF], centre[TILE - HALF :] + below], axis=0
    )


def gathered_totals(exchange, tot):
    for k in range(8):
        exchange.wait_recv(k)
    bufs = exchange.dsts
    lane = lanes(TILE)
    right = with_corners(bufs[2][...], bufs[4][...], bufs[6][...])
    left = with_corners(bufs[3][...], bufs[5][...], bufs[7][...])
    rights = (right, half_turn(right))
    lefts = (left, half_turn(left))
    parts = []
    for part in range(2):
        panels = []
        for panel in range(2):
            centre = tot[part, 1 + panel, pl.ds(HALF, TILE), :]
            centre = with_vertical(centre, bufs[0][part, panel], bufs[1][part, panel])
            extra = jnp.where(lane < HALF, lefts[part], 0.0) if panel == 0 else jnp.where(lane >= HALF, rights[part], 0.0)
            panels.append(centre + extra)
        parts.append(panels)
    return parts


def gathered_weights(exchange, wgt):
    for k in range(8):
        exchange.wait_recv(k)
    bufs = exchange.dsts
    lane = lanes(TILE)
    right = jnp.concatenate([bufs[2][...], half_turn(bufs[2][...])], axis=0)
    left = jnp.concatenate([bufs[3][...], half_turn(bufs[3][...])], axis=0)
    right = with_corners(right, bufs[4][...], bufs[6][...])
    left = with_corners(left, bufs[5][...], bufs[7][...])
    panels = []
    for panel in range(2):
        centre = with_vertical(wgt[1 + panel, pl.ds(HALF, TILE), :], bufs[0][panel], bufs[1][panel])
        extra = jnp.where(lane < HALF, left, 0.0) if panel == 0 else jnp.where(lane >= HALF, right, 0.0)
        panels.append(centre + extra)
    return panels


def margins_kernel(field, ext, *refs):
    exchange, (own, left, right, arrived) = as_exchange(refs[:10]), refs[10:]
    loads = []
    for part in range(2):
        for panel in range(2):
            src = field.at[part, :, pl.ds(panel * SIZE, SIZE)]
            loads.append(pltpu.make_async_copy(src, own.at[part, panel], arrived.at[part * 2 + panel]))
            loads[-1].start()
    barrier = pltpu.get_barrier_semaphore()
    count = signal_neighbours(barrier)
    exchange.clear_missing()
    for load in loads:
        load.wait()
    pack_margins(own, left, right)
    pl.semaphore_wait(barrier, count)
    srcs = send_margins(exchange, own, left, right)
    for part in range(2):
        for panel in range(2):
            ext[part, 1 + panel, pl.ds(HALF, TILE), :] = own[part, panel]
    fill_extended(exchange, ext)
    for k in range(8):
        exchange.wait_send(k, srcs[k])


def middle_kernel(tot, wgt, ext, probe, new_ext, den, *refs):
    totals, weights, margins = (as_exchange(refs[i : i + 10]) for i in (0, 10, 20))
    tot_left, tot_right, wgt_left, wgt_right, own, left, right = refs[30:]
    barrier = pltpu.get_barrier_semaphore()
    count = signal_neighbours(barrier)
    for exchange in (totals, weights, margins):
        exchange.clear_missing()
    pack_totals(tot, tot_left, tot_right)
    pack_weights(wgt, wgt_left, wgt_right)
    pl.semaphore_wait(barrier, count)
    tot_srcs = send_totals(totals, tot, tot_left, tot_right)
    wgt_srcs = send_weights(weights, wgt, wgt_left, wgt_right)
    power = probe[0, 0] ** 2 + probe[0, 1] ** 2 + probe[1, 0] ** 2 + probe[1, 1] ** 2
    regular = 0.1 * jnp.max(jnp.max(power, axis=0, keepdims=True), axis=1, keepdims=True) + EPSILON
    numer = gathered_totals(totals, tot)
    weight = gathered_weights(weights, wgt)
    centre = pl.ds(HALF, TILE)
    for panel in range(2):
        divisor = weight[panel] + regular
        den[panel] = divisor
        for part in range(2):
            value = (numer[part][panel] + regular * ext[part, 1 + panel, centre, :]) / divisor
            own[part, panel] = value
            new_ext[part, 1 + panel, centre, :] = value
    pack_margins(own, left, right)
    srcs = send_margins(margins, own, left, right)
    fill_extended(margins, new_ext)
    for k in range(8):
        totals.wait_send(k, tot_srcs[k])
        weights.wait_send(k, wgt_srcs[k])
        margins.wait_send(k, srcs[k])


FAR_FIRST = sorted(
    range(XS * YS), key=lambda d: -(min(d // YS, XS - d // YS) + min(d % YS, YS - d % YS))
)
SHARE = 4 * SIZE // (2 * XS * YS)


def last_kernel(tot, den, ext, probe, grad_a, grad_b, field, probe_new, *refs):
    totals = as_exchange(refs[:10])
    (tot_left, tot_right, total, from_core, half, from_plane, piece, from_line, fresh,
     core_send, core_recv, plane_send, plane_recv, line_send, line_recv,
     spread_send, spread_recv, back_send, back_recv) = refs[10:]
    row, col = lax.axis_index("row"), lax.axis_index("col")
    y, core = row // 2, row % 2
    x, z = col // ZS, col % ZS
    place = x * YS + y

    def plane_place(step_x, step_y):
        return (x + step_x + XS) % XS * YS + (y + step_y + YS) % YS

    def in_plane(d):
        other = plane_place(d // YS, d % YS)
        return other, ((other % YS) * 2 + core, (other // YS) * ZS + z)

    def source_in_plane(d):
        return plane_place(-(d // YS), -(d % YS))

    def in_line(d):
        other = (z + d) % ZS
        return other, (row, x * ZS + other)

    partner = (y * 2 + (1 - core), col)
    barrier = pltpu.get_barrier_semaphore()
    count = signal_neighbours(barrier)
    pl.semaphore_signal(barrier, 1, device_id=partner, device_id_type=MESH)
    for d in range(1, XS * YS):
        pl.semaphore_signal(barrier, 1, device_id=in_plane(d)[1], device_id_type=MESH)
    for d in range(1, ZS):
        pl.semaphore_signal(barrier, 1, device_id=in_line(d)[1], device_id_type=MESH)
    totals.clear_missing()
    for part in range(2):
        for mode in range(2):
            rows = pl.ds((part * 2 + mode) * SIZE, SIZE)
            total[rows, :] = grad_a[part, mode] + grad_b[part, mode]
    pack_totals(tot, tot_left, tot_right)
    pl.semaphore_wait(barrier, count + 1 + (XS * YS - 1) + (ZS - 1))

    def remote(src, dst, send, recv, where):
        return pltpu.make_async_remote_copy(src, dst, send, recv, device_id=where, device_id_type=MESH)

    middle = 2 * SIZE
    mine = pl.multiple_of(core * middle, middle)
    theirs = pl.multiple_of((1 - core) * middle, middle)

    def share_of(start, d):
        other, _ = in_plane(d)
        return pl.ds(pl.multiple_of(start + other * SHARE, SHARE), SHARE)

    def swap_copy(d):
        return remote(total.at[share_of(theirs, d)], from_core.at[share_of(0, d)], core_send.at[d], core_recv.at[d], partner)

    for d in FAR_FIRST:
        swap_copy(d).start()
    tot_srcs = send_totals(totals, tot, tot_left, tot_right)

    def plane_copy(d):
        _, where = in_plane(d)
        return remote(half.at[share_of(0, d)], from_plane.at[d], plane_send.at[d], plane_recv.at[d], where)

    for d in FAR_FIRST:
        swap_copy(d).wait_recv()
        half[share_of(0, d), :] = total[share_of(mine, d), :] + from_core[share_of(0, d), :]
        if d:
            plane_copy(d).start()

    share = half[pl.ds(pl.multiple_of(place * SHARE, SHARE), SHARE), :]
    for d in FAR_FIRST[-2::-1]:
        plane_copy(d).wait_recv()
        share = share + from_plane[d]
    piece[...] = share
    from_line[z] = share

    def line_copy(d):
        _, where = in_line(d)
        return remote(piece, from_line.at[z], line_send.at[d], line_recv.at[d], where)

    def line_arrival(d):
        source = (z - d + ZS) % ZS
        return remote(piece, from_line.at[source], line_send.at[d], line_recv.at[d], in_line(d)[1])

    for d in sorted(range(1, ZS), key=lambda d: -min(d, ZS - d)):
        line_copy(d).start()
    numer = gathered_totals(totals, tot)
    power = probe[0:SIZE] ** 2
    for k in range(1, 4):
        power = power + probe[k * SIZE : (k + 1) * SIZE] ** 2
    regular = 0.1 * jnp.max(jnp.max(power, axis=0, keepdims=True), axis=1, keepdims=True) + EPSILON
    for part in range(2):
        for panel in range(2):
            own = ext[part, 1 + panel, pl.ds(HALF, TILE), :]
            field[part, :, panel * SIZE : (panel + 1) * SIZE] = (numer[part][panel] + regular * own) / den[panel]
    for d in range(1, ZS):
        line_arrival(d).wait_recv()
    summed = from_line[0]
    for k in range(1, ZS):
        summed = summed + from_line[k]
    rows = pl.ds(pl.multiple_of(mine + place * SHARE, SHARE), SHARE)
    slots = float(ROWS * COLS * 24)
    fresh[rows, :] = probe[rows, :] + summed / slots

    def spread_copy(d):
        _, where = in_plane(d)
        return remote(fresh.at[rows], fresh.at[rows], spread_send.at[d], spread_recv.at[d], where)

    def spread_arrival(d):
        there = pl.ds(pl.multiple_of(mine + source_in_plane(d) * SHARE, SHARE), SHARE)
        return remote(fresh.at[rows], fresh.at[there], spread_send.at[d], spread_recv.at[d], in_plane(d)[1])

    def back_copy(d, start):
        there = pl.ds(pl.multiple_of(start + source_in_plane(d) * SHARE, SHARE), SHARE)
        return remote(fresh.at[there], fresh.at[there], back_send.at[d], back_recv.at[d], partner)

    for d in FAR_FIRST[:-1]:
        spread_copy(d).start()
    back_copy(0, mine).start()
    for d in FAR_FIRST[-2::-1]:
        spread_arrival(d).wait_recv()
        back_copy(d, mine).start()
    for d in range(XS * YS):
        back_copy(d, theirs).wait_recv()
    probe_new[...] = fresh[...]
    for d in range(XS * YS):
        swap_copy(d).wait_send()
        back_copy(d, mine).wait_send()
    for d in range(1, XS * YS):
        plane_copy(d).wait_send()
        spread_copy(d).wait_send()
    for d in range(1, ZS):
        line_copy(d).wait_send()
    for k in range(8):
        totals.wait_send(k, tot_srcs[k])


def split(x):
    high = x.astype(BF16)
    return high, (x - high.astype(F32)).astype(BF16)


def turned(y):
    return jnp.concatenate(
        [
            jnp.concatenate([y[:SIZE, :SIZE], y[SIZE:, :SIZE]], axis=1),
            jnp.concatenate([y[:SIZE, SIZE:], y[SIZE:, SIZE:]], axis=1),
        ],
        axis=0,
    )


def visit_kernel(with_weight, *refs):
    unit = (2 * SIZE, 2 * SIZE)
    accumulators = [pltpu.ACC(u)(unit, F32) for _ in range(4) for u in range(PAIR)]
    pl.run_scoped(functools.partial(visit_slots, with_weight, refs), *accumulators)


def visit_slots(with_weight, refs, *accumulators):
    off, cnt, ext, probe, table, amp, tot, *refs = refs
    if with_weight:
        wgt, *refs = refs
        wgt[...] = jnp.zeros_like(wgt)
    grad, spread, power, *pairs, kept = refs
    exits, first, second, third = (tuple(pairs[i : i + 2]) for i in (0, 2, 4, 6))
    acc_a, acc_b, acc_c, acc_d = (accumulators[i : i + PAIR] for i in range(0, 4 * PAIR, PAIR))
    tot[...] = jnp.zeros_like(tot)
    grad[...] = jnp.zeros_like(grad)
    spread[...] = jnp.zeros_like(spread)
    if with_weight:
        power[...] = probe[0, 0] ** 2 + probe[0, 1] ** 2 + probe[1, 0] ** 2 + probe[1, 1] ** 2
    count = cnt[0, 0]
    slots = amp.shape[0]
    lane = lanes(SIZE)
    both = range(PAIR)

    def clamped(index, u):
        return jnp.minimum(index * PAIR + u, slots - 1)

    def live(index, u):
        return (index * PAIR + u < count).astype(F32)

    def corner(index, u):
        slot = clamped(index, u)
        row = off[0, slot] + HALF
        col = off[1, slot] + SIZE
        return row, col // SIZE, col % SIZE

    def on_rows(acc, which, terms, u):
        high, low = terms
        pltpu.matmul_push_rhs(high[u], 0, u)
        pltpu.matmul_push_rhs(low[u], 1, u)
        pltpu.matmul_acc_lhs(acc[u], table[2 * which], load_staged_rhs=0)
        pltpu.matmul_acc_lhs(acc[u], table[2 * which + 1])
        pltpu.matmul_acc_lhs(acc[u], table[2 * which], load_staged_rhs=1)

    def on_columns(acc, which, terms, u):
        high, low = terms
        pltpu.matmul_push_rhs(table[2 * which], 0, u)
        pltpu.matmul_push_rhs(table[2 * which + 1], 1, u)
        pltpu.matmul_acc_lhs(acc[u], high[u], load_staged_rhs=0)
        pltpu.matmul_acc_lhs(acc[u], low[u])
        pltpu.matmul_acc_lhs(acc[u], high[u], load_staged_rhs=1)

    def keep_terms(terms, u, value):
        terms[0][u], terms[1][u] = split(value)

    def fetch(index, u):
        row, panel, shift = corner(index, u)
        upper = lane >= shift
        back = (SIZE - shift) % SIZE
        window = []
        for part in range(2):
            near = ext[part, panel, pl.ds(row, SIZE), :]
            far = ext[part, panel + 1, pl.ds(row, SIZE), :]
            window.append(pltpu.roll(jnp.where(upper, near, far), back, 1))
        squared = window[0] * window[0] + window[1] * window[1]
        mean = jnp.sum(jnp.sum(squared, axis=0, keepdims=True), axis=1, keepdims=True) * (1.0 / SIZE**2) + EPSILON
        scale = live(index, u) / mean
        for m in range(2):
            pr, pi = probe[0, m], probe[1, m]
            block = pl.ds(m * SIZE, SIZE)
            for rows, value in (
                (pl.ds(0, SIZE), pr * window[0] - pi * window[1]),
                (pl.ds(SIZE, SIZE), pr * window[1] + pi * window[0]),
            ):
                high, low = split(value)
                exits[0][u, rows, block] = high
                exits[1][u, rows, block] = low
        place = index % 3
        kept[place, u, 0] = window[0] * scale
        kept[place, u, 1] = window[1] * scale
        spread[...] += squared * scale

    def rescale(index, u):
        z = pltpu.matmul_pop(acc_b[u])
        sq = z * z
        level = sq[:SIZE, :SIZE] + sq[:SIZE, SIZE:] + sq[SIZE:, :SIZE] + sq[SIZE:, SIZE:]
        factor = amp[clamped(index, u)] * (jnp.minimum(lax.rsqrt(level), 1.0) * live(index, u))
        wide = jnp.concatenate([factor, factor], axis=1)
        keep_terms(second, u, jnp.concatenate([z[:SIZE] * wide, z[SIZE:] * wide], axis=0))

    def place(index, u):
        row, panel, shift = corner(index, u)
        upper = lane >= shift
        revised = pltpu.matmul_pop(acc_d[u])
        wr, wi = kept[index % 3, u, 0], kept[index % 3, u, 1]
        real, imag, terms = 0.0, 0.0, []
        for m in range(2):
            vr = revised[:SIZE, m * SIZE : (m + 1) * SIZE]
            vi = revised[SIZE:, m * SIZE : (m + 1) * SIZE]
            pr, pi = probe[0, m], probe[1, m]
            real = real + (pr * vr + pi * vi)
            imag = imag + (pr * vi - pi * vr)
            terms.append((wr * vr + wi * vi, wr * vi - wi * vr))
        add_at(tot.at[0], row, panel, shift, upper, real)
        add_at(tot.at[1], row, panel, shift, upper, imag)
        return terms

    def add_at(ref, row, panel, shift, upper, value):
        moved = pltpu.roll(value, shift, 1)
        near, far = ref.at[panel, pl.ds(row, SIZE), :], ref.at[panel + 1, pl.ds(row, SIZE), :]
        pltpu.store(near, near[...] + moved, mask=upper)
        pltpu.store(far, far[...] + moved, mask=jnp.logical_not(upper))

    def weigh(index, u):
        if with_weight:
            row, panel, shift = corner(index, u)
            add_at(wgt, row, panel, shift, lane >= shift, power[...] * live(index, u))

    def add_terms(terms):
        for m in range(2):
            for part in range(2):
                grad[part, m] += terms[0][m][part] + terms[1][m][part]

    pairs_live = (count + PAIR - 1) // PAIR
    for u in both:
        fetch(0, u)
    for u in both:
        on_rows(acc_a, 1, exits, u)
    for u in both:
        fetch(1, u)
    for u in both:
        keep_terms(first, u, turned(pltpu.matmul_pop(acc_a[u])))
    for u in both:
        on_columns(acc_b, 0, first, u)
    for u in both:
        on_rows(acc_a, 1, exits, u)
    for u in both:
        weigh(0, u)
    for u in both:
        rescale(0, u)

    def slotwise(index, carry):
        terms = []
        for u in both:
            keep_terms(first, u, turned(pltpu.matmul_pop(acc_a[u])))
            on_columns(acc_c, 1, second, u)
            fetch(index + 1, u)
            on_columns(acc_b, 0, first, u)
            keep_terms(third, u, turned(pltpu.matmul_pop(acc_c[u])))
            on_rows(acc_d, 0, third, u)
            weigh(index, u)
            rescale(index, u)
            on_rows(acc_a, 1, exits, u)
            terms.append(place(index - 1, u))
        add_terms(terms)
        return carry

    def pairwise(index, carry):
        for u in both:
            keep_terms(first, u, turned(pltpu.matmul_pop(acc_a[u])))
        for u in both:
            on_columns(acc_c, 1, second, u)
        fetch(index + 1, 0)
        for u in both:
            keep_terms(third, u, turned(pltpu.matmul_pop(acc_c[u])))
        for u in both:
            on_columns(acc_b, 0, first, u)
        fetch(index + 1, 1)
        for u in both:
            rescale(index, u)
        for u in both:
            on_rows(acc_d, 0, third, u)
        terms = [place(index - 1, u) for u in both]
        for u in both:
            on_rows(acc_a, 1, exits, u)
        add_terms(terms)
        return carry

    lax.fori_loop(1, pairs_live, slotwise if with_weight else pairwise, 0)
    for u in both:
        on_columns(acc_c, 1, second, u)
    for u in both:
        keep_terms(third, u, turned(pltpu.matmul_pop(acc_c[u])))
    for u in both:
        on_rows(acc_d, 0, third, u)
    add_terms([place(pairs_live - 1, u) for u in both])
    for u in both:
        keep_terms(first, u, pltpu.matmul_pop(acc_a[u]))
    for part in range(2):
        for m in range(2):
            grad[part, m] -= probe[part, m] * spread[...]


def store_kernel(field, probe, field_out, probe_out, done):
    copies = [
        pltpu.make_async_copy(field.at[0], field_out.at[0], done.at[0]),
        pltpu.make_async_copy(field.at[1], field_out.at[1], done.at[1]),
        pltpu.make_async_copy(probe, probe_out, done.at[2]),
    ]
    for copy in copies:
        copy.start()
    for copy in copies:
        copy.wait()


def store(field, probe):
    hbm = pl.BlockSpec(memory_space=pltpu.HBM)
    return pl.pallas_call(
        store_kernel,
        out_shape=[shape(*field.shape), shape(*probe.shape)],
        in_specs=[VMEM, VMEM],
        out_specs=[hbm, hbm],
        scratch_shapes=[pltpu.SemaphoreType.DMA((3,))],
        compiler_params=pltpu.CompilerParams(vmem_limit_bytes=32 << 20),
        name="store",
    )(field, probe)


def shape(*dims):
    return jax.ShapeDtypeStruct(dims, F32)


def visit(with_weight, off, cnt, ext, probe, table, amp):
    outs = [shape(2, 4, EXT, SIZE)] + [shape(4, EXT, SIZE)] * with_weight + [shape(2, 2, SIZE, SIZE)]
    return pl.pallas_call(
        functools.partial(visit_kernel, with_weight),
        out_shape=outs,
        in_specs=[SMEM, SMEM, VMEM, VMEM, VMEM, VMEM],
        out_specs=[VMEM] * len(outs),
        scratch_shapes=[pltpu.VMEM((SIZE, SIZE), F32)] * 2
        + [pltpu.VMEM((PAIR, 2 * SIZE, 2 * SIZE), BF16)] * 8
        + [pltpu.VMEM((3, PAIR, 2, SIZE, SIZE), F32)],
        compiler_params=pltpu.CompilerParams(vmem_limit_bytes=32 << 20),
        name="visit",
    )(off, cnt, ext, probe, table, amp)


def remote_call(kernel, name, collective_id, outs, scratch, *args, specs=None, cost=None):
    return pl.pallas_call(
        kernel,
        out_shape=outs,
        in_specs=specs or [VMEM] * len(args),
        out_specs=jax.tree.map(lambda _: VMEM, outs),
        scratch_shapes=scratch,
        compiler_params=pltpu.CompilerParams(
            collective_id=collective_id, has_side_effects=True, vmem_limit_bytes=32 << 20
        ),
        cost_estimate=cost,
        name=name,
    )(*args)


def local(field, probe, amplitudes, offsets, counts):
    amp = amplitudes[0, 0]
    offsets = offsets[0, 0].T
    table = jnp.asarray(dft_tables())
    buffer = pltpu.VMEM((TILE, SIZE), F32)
    long = pltpu.VMEM((EXT, SIZE), F32)
    own = pltpu.VMEM((2, 2, TILE, SIZE), F32)
    ext = remote_call(
        margins_kernel, "margins", 0, shape(2, 4, EXT, SIZE),
        FIELD_SCRATCH + [own, buffer, buffer, pltpu.SemaphoreType.DMA((4,))],
        pltpu.with_memory_space_constraint(field, pltpu.HBM), specs=[pl.BlockSpec(memory_space=pltpu.HBM)], cost=pl.CostEstimate(flops=10**10, bytes_accessed=10**7, transcendentals=0),
    )
    tot, wgt, grad_a = visit(True, offsets, counts, ext, probe, table, amp)
    packed = pltpu.VMEM((SIZE, SIZE), F32)
    ext, den = remote_call(
        middle_kernel, "middle", 1, [shape(2, 4, EXT, SIZE), shape(2, TILE, SIZE)],
        FIELD_SCRATCH + WEIGHT_SCRATCH + FIELD_SCRATCH + [long, long, packed, packed, own, buffer, buffer],
        tot, wgt, ext, probe,
    )
    tot, grad_b = visit(False, offsets, counts, ext, probe, table, amp)
    plane, line = XS * YS, ZS
    dma = pltpu.SemaphoreType.DMA
    scratch = FIELD_SCRATCH + [
        long, long,
        pltpu.VMEM((4 * SIZE, SIZE), F32),
        pltpu.VMEM((2 * SIZE, SIZE), F32),
        pltpu.VMEM((2 * SIZE, SIZE), F32),
        pltpu.VMEM((plane, SHARE, SIZE), F32),
        pltpu.VMEM((SHARE, SIZE), F32),
        pltpu.VMEM((line, SHARE, SIZE), F32),
        pltpu.VMEM((4 * SIZE, SIZE), F32),
        *[dma((n,)) for n in (plane, plane, plane, plane, line, line, plane, plane, plane, plane)],
    ]
    field_new, probe_new = remote_call(
        last_kernel, "last", 2, [shape(2, TILE, TILE), shape(4 * SIZE, SIZE)], scratch,
        tot, den, ext, probe.reshape(4 * SIZE, SIZE), grad_a, grad_b,
    )
    return store(field_new, probe_new.reshape(2, 2, SIZE, SIZE))


def solution(mesh):
    in_specs = (
        P(None, "row", "col"),
        P(),
        P("row", "col", None, None, None),
        P("row", "col", None, None),
        P("row", "col"),
    )
    out_specs = (P(None, "row", "col"), P())
    return jax.shard_map(local, mesh=mesh, in_specs=in_specs, out_specs=out_specs, check_vma=False)
```
